32 devices in a mesh: pipe: 4 (over z), dp: 2 (over x), tensor: 4 (over y, core).
Axes of the slice: x: 2, y: 2, z: 4, core: 2. Of those that a mesh axis runs over, the one named last changes fastest.
Arguments:
- acts: bfloat16 [4, 4, 128, 8192], P('pipe', None, 'dp', 'tensor'), may hold values from -6 to 6
- w_in: bfloat16 [4, 8192, 512], P('pipe', 'tensor', 'dp'), may hold values from -0.0625 to 0.0625
- w_out: bfloat16 [4, 512, 8192], P('pipe', 'dp', 'tensor'), may hold values from -0.25 to 0.25
- top_grad: bfloat16 [4, 128, 8192], P(None, 'dp', 'tensor'), may hold values from -6 to 6
Outputs:
- grad_input: bfloat16 [4, 4, 128, 8192], P('pipe', None, 'dp', 'tensor')
- grad_w_in: bfloat16 [4, 8192, 512], P('pipe', 'tensor', 'dp')
- grad_w_out: bfloat16 [4, 512, 8192], P('pipe', 'dp', 'tensor')
The draws below stay inside these ranges and needn't reach their ends.
All inputs are finite; a program needn't handle non-finite values.
Results may differ from the reference program's by a relative error of at most 0.013.
Values may be sent and summed in bfloat16 or wider, within the bound.
A program may use at most 64 MiB of HBM per device.

```python
import jax
import jax.numpy as jnp
from jax import lax

D = 8192
R = 512
M = 4
TOKM = 64
TOKENS = 128
SECTIONS = 4
N_PIPE = 4
N_DP = 2


def levels(rng, dims, cuts, least, top_value):
    loudness = 1.0
    for axis_at, parts in cuts:
        heights = jax.random.uniform(jax.random.fold_in(jax.random.fold_in(rng, 6), axis_at), (parts,), jnp.float32, least / len(cuts), top_value / len(cuts))
        loudness = loudness * jnp.repeat(jnp.exp(heights), dims[axis_at] // parts).reshape((-1,) + (1,) * (len(dims) - 1 - axis_at))
    return loudness


def bell_draw(stream_key, extent, scale, most, pieces=(), held_as=jnp.bfloat16):
    drawn = scale * jax.random.normal(stream_key, extent, jnp.float32)
    if pieces:
        drawn = drawn * levels(stream_key, extent, pieces, -0.22, 0.18)
    return jnp.clip(drawn, -most, most).astype(held_as)


def setup_inputs(seed: int = 0) -> dict:
    key_of = jax.random.split(jax.random.key(seed), 5)
    return {
        "acts": bell_draw(key_of[0], (SECTIONS, M, TOKENS, D), 1.0, 6.0, ((0, 4), (2, 2), (3, 4))),
        "w_in": bell_draw(key_of[1], (SECTIONS, D, R), D ** -0.5, 0.0625, ((0, 4), (1, 4), (2, 2))),
        "w_out": bell_draw(key_of[2], (SECTIONS, R, D), R ** -0.5, 0.25, ((0, 4), (1, 2), (2, 4))),
        "top_grad": bell_draw(key_of[3], (M, TOKENS, D), 1.0, 6.0, ((1, 2), (2, 4))),
    }


def silu_slope(value):
    sig = jax.nn.sigmoid(value)
    return sig * (1.0 + value * (1.0 - sig))


def block_sum(left, right):
    left4 = left.reshape(M, N_DP, TOKM, left.shape[-1])
    right4 = right.reshape(M, N_DP, TOKM, right.shape[-1])

    def step_fn(total, index):
        left_b = lax.dynamic_index_in_dim(left4, index, 1, keepdims=False).reshape(M * TOKM, -1)
        right_b = lax.dynamic_index_in_dim(right4, index, 1, keepdims=False).reshape(M * TOKM, -1)
        part = jnp.dot(left_b.T, right_b, preferred_element_type=jnp.float32)
        part = part.astype(jnp.bfloat16).astype(jnp.float32)
        return total + part, 0

    start = jnp.zeros((left.shape[-1], right.shape[-1]), jnp.float32)
    total, unused = lax.scan(step_fn, start, jnp.arange(N_DP, dtype=jnp.int32))
    return total.astype(jnp.bfloat16)


def reference(acts, w_in, w_out, top_grad):
    grad_now = top_grad.reshape(M * TOKENS, D)
    inputs_list = []
    w_in_list = []
    w_out_list = []
    for section in reversed(range(N_PIPE)):
        x_rows = acts[section].reshape(M * TOKENS, D).astype(jnp.float32)
        wi = w_in[section].astype(jnp.float32)
        wo = w_out[section].astype(jnp.float32)
        pre = jnp.dot(x_rows, wi, preferred_element_type=jnp.float32)
        act = jax.nn.silu(pre).astype(jnp.bfloat16)
        grad_f = grad_now.astype(jnp.float32)
        hidden = jnp.dot(grad_f, wo.T, preferred_element_type=jnp.float32)
        dpre = (hidden * silu_slope(pre)).astype(jnp.bfloat16)
        back = (grad_f + jnp.dot(dpre.astype(jnp.float32), wi.T, preferred_element_type=jnp.float32)).astype(jnp.bfloat16)
        w_in_list.append(block_sum(x_rows, dpre.astype(jnp.float32)))
        w_out_list.append(block_sum(act.astype(jnp.float32), grad_f))
        inputs_list.append(back.reshape(M, TOKENS, D))
        grad_now = back
    return jnp.stack(inputs_list[::-1]), jnp.stack(w_in_list[::-1]), jnp.stack(w_out_list[::-1])
```

```python
import functools

import jax
import jax.numpy as jnp
from jax import lax
from jax.experimental import pallas as pl
from jax.experimental.pallas import tpu as pltpu
from jax.sharding import PartitionSpec as P

MESH = pl.DeviceIdType.MESH
LAST = (((1,), (1,)), ((), ()))
FIRST = (((0,), (0,)), ((), ()))
STEP = 16
LAG = 2


def silu_slope(value):
    sig = jax.nn.sigmoid(value)
    return sig * (1.0 + value * (1.0 - sig))


def dot(left, right, dims):
    return lax.dot_general(left, right, dims, preferred_element_type=jnp.float32)


def mm(left, right):
    return jnp.dot(left, right, preferred_element_type=jnp.float32)


def remote(src, dst, send, recv, where):
    return pltpu.make_async_remote_copy(
        src_ref=src, dst_ref=dst, send_sem=send, recv_sem=recv,
        device_id=where, device_id_type=MESH,
    )


def paired(
    pipes, parts,
    x_hbm, wi_hbm, wo_hbm, top_hbm,
    back_ref, gin_ref, gout_ref,
    x_own, x_other, wi_own, wi_other, wo_own, wot, wit, g_own, g_other,
    pre_part, pre_recv, pre_full, slope, act, act_other, dpre, dpre_other,
    hid_own, hid_send, hid_recv, gin_acc, gout_acc,
    load_sem, bulk_ss, bulk_rs, pre_ss, pre_rs, full_ss, full_rs,
    hid_ss, hid_rs, g_ss, g_rs, gx_ss, gx_rs, dx_ss, dx_rs,
):
    rows, width = x_own.shape
    own = wi_own.shape[1]
    count = rows // STEP
    share = rows // parts
    section = lax.axis_index("pipe")
    me = lax.axis_index("tensor")
    first = section == pipes - 1
    last = section == 0
    below = jnp.maximum(section - 1, 0)
    above = jnp.minimum(section + 1, pipes - 1)
    peers = [lax.rem(me + d, parts) for d in range(1, parts)]
    partner = {"dp": 1 - lax.axis_index("dp")}

    barrier = pltpu.get_barrier_semaphore()
    for peer in peers:
        pl.semaphore_signal(barrier, inc=1, device_id={"tensor": peer}, device_id_type=MESH)
    pl.semaphore_signal(barrier, inc=1, device_id=partner, device_id_type=MESH)

    @pl.when(section > 0)
    def _():
        pl.semaphore_signal(barrier, inc=1, device_id={"pipe": below}, device_id_type=MESH)

    @pl.when(section < pipes - 1)
    def _():
        pl.semaphore_signal(barrier, inc=1, device_id={"pipe": above}, device_id_type=MESH)

    loads = [
        pltpu.make_async_copy(src, dst, load_sem.at[i])
        for i, (src, dst) in enumerate([(x_hbm, x_own), (wi_hbm, wi_own), (wo_hbm, wo_own), (top_hbm, g_own)])
    ]
    for copy in loads[:3]:
        copy.start()

    @pl.when(first)
    def _():
        loads[3].start()

    beside = jnp.minimum(section, 1) + jnp.minimum(pipes - 1 - section, 1)
    pl.semaphore_wait(barrier, parts + beside)

    wi_copy = remote(wi_hbm, wi_other, bulk_ss.at[0], bulk_rs.at[0], partner)
    wo_copy = remote(wot.at[0], wot.at[1], bulk_ss.at[1], bulk_rs.at[1], partner)
    x_copy = remote(x_hbm, x_other, bulk_ss.at[2], bulk_rs.at[2], partner)
    act_copy = remote(act.at[1], act_other, bulk_ss.at[3], bulk_rs.at[3], partner)
    wi_copy.start()

    loads[2].wait()

    def turn_out(b, carry):
        cols = pl.ds(pl.multiple_of(b * 256, 256), 256)
        wot[0, cols, :] = wo_own[:, cols].T
        return carry

    lax.fori_loop(0, width // 256, turn_out, 0)
    wo_copy.start()
    x_copy.start()

    def pre_copies(h):
        return [
            remote(
                pre_part.at[h, pl.ds(peer * share, share)], pre_recv.at[h, d],
                pre_ss.at[h, d], pre_rs.at[h, d], {"tensor": peer},
            )
            for d, peer in enumerate(peers)
        ]

    def full_copies(h):
        mine = pl.ds(me * share, share)
        return [
            remote(
                pre_full.at[h, mine], pre_full.at[h, mine],
                full_ss.at[h, d], full_rs.at[h, d], {"tensor": peer},
            )
            for d, peer in enumerate(peers)
        ]

    def turn_in(h, src):
        def body(b, carry):
            cols = pl.ds(pl.multiple_of(b * 256, 256), 256)
            wit[h, :, cols] = src[cols, :].T
            return carry

        lax.fori_loop(0, width // 256, body, 0)

    def pre_start(h, src):
        pre_part[h] = mm(x_own[...], src[...])
        for copy in pre_copies(h):
            copy.start()

    def pre_sum(h):
        for copy in pre_copies(h):
            copy.wait_recv()
        mine = pl.ds(pl.multiple_of(me * share, share), share)
        total = pre_part[h, mine, :]
        for d in range(parts - 1):
            total = total + pre_recv[h, d]
        pre_full[h, mine, :] = total
        for copy in full_copies(h):
            copy.start()

    def pre_end(h):
        for copy in full_copies(h):
            copy.wait_recv()
        value = pre_full[h]
        slope[h] = silu_slope(value)
        act[h] = jax.nn.silu(value).astype(jnp.bfloat16)

    loads[0].wait()
    loads[1].wait()
    pre_start(0, wi_own)
    turn_in(0, wi_own)
    pre_sum(0)
    pre_end(0)
    wi_copy.wait_recv()
    pre_start(1, wi_other)
    turn_in(1, wi_other)
    pre_sum(1)
    pre_end(1)
    act_copy.start()

    @pl.when(first)
    def _():
        loads[3].wait()

    wo_copy.wait_recv()

    def rows_of(k):
        return pl.ds(pl.multiple_of(k * STEP, STEP), STEP)

    def g_copy(k):
        return remote(back_ref.at[rows_of(k)], g_own.at[rows_of(k)], g_ss.at[k], g_rs.at[k], {"pipe": below})

    def gx_copy(k):
        return remote(g_own.at[rows_of(k)], g_other.at[rows_of(k)], gx_ss.at[k], gx_rs.at[k], partner)

    def dx_copy(k):
        return remote(dpre.at[1, rows_of(k)], dpre_other.at[rows_of(k)], dx_ss.at[k], dx_rs.at[k], partner)

    def hid_copies(k):
        return [
            remote(hid_send.at[k], hid_recv.at[k, d], hid_ss.at[k, d], hid_rs.at[k, d], {"tensor": peer})
            for d, peer in enumerate(peers)
        ]

    def hidden_now(k):
        @pl.when(section < pipes - 1)
        def _():
            g_copy(k).wait_recv()

        gx_copy(k).start()
        g_now = g_own[rows_of(k), :]
        for h in range(2):
            part = mm(g_now, wot[h])
            hid_own[k, h] = part
            hid_send[k, h] = part.astype(jnp.bfloat16)
        for copy in hid_copies(k):
            copy.start()

    def back_now(k):
        for copy in hid_copies(k):
            copy.wait_recv()
        total = g_own[rows_of(k), :].astype(jnp.float32)
        for h in range(2):
            hidden = hid_own[k, h]
            for d in range(parts - 1):
                hidden = hidden + hid_recv[k, d, h].astype(jnp.float32)
            slice_d = (hidden * slope[h, rows_of(k), :]).astype(jnp.bfloat16)
            dpre[h, rows_of(k), :] = slice_d
            total = total + mm(slice_d, wit[h])
        back_ref[rows_of(k), :] = total.astype(jnp.bfloat16)

        @pl.when(section > 0)
        def _():
            g_copy(k).start()

        dx_copy(k).start()

    def chain(k, carry):
        @pl.when(k < count)
        def _():
            hidden_now(k)

        @pl.when(k >= LAG)
        def _():
            back_now(k - LAG)

        return carry

    lax.fori_loop(0, count + LAG, chain, 0)

    tile = 512

    def own_grads(c, carry):
        cols = pl.ds(pl.multiple_of(c * tile, tile), tile)
        gin_acc[cols, :] = dot(x_own[:, cols], dpre[0], FIRST)
        gout_acc[:, cols] = dot(act[0], g_own[:, cols], FIRST)
        return carry

    lax.fori_loop(0, width // tile, own_grads, 0)
    x_copy.wait_recv()
    act_copy.wait_recv()

    group = 64
    per = group // STEP

    def wait_group(j, carry):
        def one(i, inner):
            gx_copy(j * per + i).wait_recv()
            return inner

        lax.fori_loop(0, per, one, 0)
        r = pl.ds(pl.multiple_of(j * group, group), group)

        def cols_of(c, inner):
            cols = pl.ds(pl.multiple_of(c * tile, tile), tile)
            gout_acc[:, cols] += dot(act_other[r, :], g_other[r, cols], FIRST)
            return inner

        lax.fori_loop(0, width // tile, cols_of, 0)
        return carry

    lax.fori_loop(0, rows // group, wait_group, 0)

    def wait_dx(k, carry):
        dx_copy(k).wait_recv()
        return carry

    lax.fori_loop(0, count, wait_dx, 0)

    def end_grads(c, carry):
        cols = pl.ds(pl.multiple_of(c * tile, tile), tile)
        gin_ref[cols, :] = (gin_acc[cols, :] + dot(x_other[:, cols], dpre_other[...], FIRST)).astype(jnp.bfloat16)
        gout_ref[:, cols] = gout_acc[:, cols].astype(jnp.bfloat16)
        return carry

    lax.fori_loop(0, width // tile, end_grads, 0)

    for copy in [wi_copy, wo_copy, x_copy, act_copy]:
        copy.wait_send()
    for h in range(2):
        for copy in pre_copies(h) + full_copies(h):
            copy.wait_send()

    def drain(k, carry):
        gx_copy(k).wait_send()
        dx_copy(k).wait_send()
        for copy in hid_copies(k):
            copy.wait_send()

        @pl.when(section > 0)
        def _():
            g_copy(k).wait_send()

        return carry

    lax.fori_loop(0, count, drain, 0)


def pair_call(saved, w_in_now, w_out_now, top):
    pipes = lax.axis_size("pipe")
    parts = lax.axis_size("tensor")
    rows, width = saved.shape
    own = w_in_now.shape[1]
    count = rows // STEP
    share = rows // parts
    others = parts - 1
    bf, f32 = jnp.bfloat16, jnp.float32
    dma = pltpu.SemaphoreType.DMA
    vmem = pl.BlockSpec(memory_space=pltpu.VMEM)
    anywhere = pl.BlockSpec(memory_space=pl.ANY)
    return pl.pallas_call(
        functools.partial(paired, pipes, parts),
        out_shape=(
            jax.ShapeDtypeStruct((rows, width), bf),
            jax.ShapeDtypeStruct((width, own), bf),
            jax.ShapeDtypeStruct((own, width), bf),
        ),
        in_specs=[anywhere] * 4,
        out_specs=(vmem,) * 3,
        scratch_shapes=[
            pltpu.VMEM((rows, width), bf),
            pltpu.VMEM((rows, width), bf),
            pltpu.VMEM((width, own), bf),
            pltpu.VMEM((width, own), bf),
            pltpu.VMEM((own, width), bf),
            pltpu.VMEM((2, width, own), bf),
            pltpu.VMEM((2, own, width), bf),
            pltpu.VMEM((rows, width), bf),
            pltpu.VMEM((rows, width), bf),
            pltpu.VMEM((2, rows, own), f32),
            pltpu.VMEM((2, others, share, own), f32),
            pltpu.VMEM((2, rows, own), f32),
            pltpu.VMEM((2, rows, own), f32),
            pltpu.VMEM((2, rows, own), bf),
            pltpu.VMEM((rows, own), bf),
            pltpu.VMEM((2, rows, own), bf),
            pltpu.VMEM((rows, own), bf),
            pltpu.VMEM((count, 2, STEP, own), f32),
            pltpu.VMEM((count, 2, STEP, own), bf),
            pltpu.VMEM((count, others, 2, STEP, own), bf),
            pltpu.VMEM((width, own), f32),
            pltpu.VMEM((own, width), f32),
            dma((4,)), dma((4,)), dma((4,)),
            dma((2, others)), dma((2, others)), dma((2, others)), dma((2, others)),
            dma((count, others)), dma((count, others)),
            dma((count,)), dma((count,)), dma((count,)), dma((count,)), dma((count,)), dma((count,)),
        ],
        compiler_params=pltpu.CompilerParams(
            collective_id=0, has_side_effects=True, vmem_limit_bytes=48 * 1024 * 1024
        ),
    )(saved, w_in_now, w_out_now, top)


def chain(
    pipes, parts, pair, chunks,
    x_ref, wi_ref, wo_ref, top_ref,
    back_ref, pin_ref, pout_ref,
    g_buf, pre_send, pre_recv, act_buf, hid_send, hid_recv, dpre_buf, slope_buf,
    pre_ss, pre_rs, act_ss, act_rs, hid_ss, hid_rs, dp_ss, dp_rs, g_ss, g_rs,
    *across,
):
    micro, rows, width = x_ref.shape
    own = wi_ref.shape[1]
    halves = 2 if pair else 1
    per = parts // halves
    quarter = own // per
    step_w = width // chunks
    section = lax.axis_index("pipe")
    me = lax.axis_index("tensor")
    first = section == pipes - 1
    below = jnp.maximum(section - 1, 0)
    above = jnp.minimum(section + 1, pipes - 1)
    peers = [lax.rem(me + d, parts) for d in range(1, parts)]

    barrier = pltpu.get_barrier_semaphore()
    for peer in peers:
        pl.semaphore_signal(barrier, inc=1, device_id={"tensor": peer}, device_id_type=MESH)
    if pair:
        partner = {"dp": 1 - lax.axis_index("dp")}
        pl.semaphore_signal(barrier, inc=1, device_id=partner, device_id_type=MESH)

    @pl.when(section > 0)
    def _():
        pl.semaphore_signal(barrier, inc=1, device_id={"pipe": below}, device_id_type=MESH)

    @pl.when(section < pipes - 1)
    def _():
        pl.semaphore_signal(barrier, inc=1, device_id={"pipe": above}, device_id_type=MESH)

    beside = jnp.minimum(section, 1) + jnp.minimum(pipes - 1 - section, 1)
    pl.semaphore_wait(barrier, parts - 1 + halves - 1 + beside)

    def remote(src, dst, send, recv, where):
        return pltpu.make_async_remote_copy(
            src_ref=src, dst_ref=dst, send_sem=send, recv_sem=recv,
            device_id=where, device_id_type=MESH,
        )

    wi_halves, wo_halves = [wi_ref], [wo_ref]
    if pair:
        wi_other, wo_other, x_other, g_other, dpre_other, act_other, one_ss, one_rs, gx_ss, gx_rs, dx_ss, dx_rs = across
        wi_halves.append(wi_other)
        wo_halves.append(wo_other)
        wi_copy = remote(wi_ref, wi_other, one_ss.at[0], one_rs.at[0], partner)
        wo_copy = remote(wo_ref, wo_other, one_ss.at[1], one_rs.at[1], partner)
        x_copy = remote(x_ref, x_other, one_ss.at[2], one_rs.at[2], partner)
        actx_copy = remote(act_buf.at[pl.ds(per, per)], act_other, one_ss.at[3], one_rs.at[3], partner)
        gx_copies = [remote(g_buf.at[m], g_other.at[m], gx_ss.at[m], gx_rs.at[m], partner) for m in range(micro)]
        dx_copies = [
            remote(dpre_buf.at[m, pl.ds(per, per)], dpre_other.at[m], dx_ss.at[m], dx_rs.at[m], partner)
            for m in range(micro)
        ]
        wi_copy.start()

    @pl.when(first)
    def _():
        g_buf[...] = top_ref[...]

    pre_copies = [
        remote(pre_send.at[peer], pre_recv.at[d], pre_ss.at[d], pre_rs.at[d], {"tensor": peer})
        for d, peer in enumerate(peers)
    ]
    hid_copies = [
        [
            remote(hid_send.at[m, peer], hid_recv.at[m, d], hid_ss.at[m, d], hid_rs.at[m, d], {"tensor": peer})
            for d, peer in enumerate(peers)
        ]
        for m in range(micro)
    ]
    dp_copies = [
        [
            remote(dpre_buf.at[m, me], dpre_buf.at[m, me], dp_ss.at[m, d], dp_rs.at[m, d], {"tensor": peer})
            for d, peer in enumerate(peers)
        ]
        for m in range(micro)
    ]
    act_copies = [
        remote(act_buf.at[me], act_buf.at[me], act_ss.at[d], act_rs.at[d], {"tensor": peer})
        for d, peer in enumerate(peers)
    ]
    g_copies = [
        [
            remote(
                back_ref.at[m, :, pl.ds(c * step_w, step_w)], g_buf.at[m, :, pl.ds(c * step_w, step_w)],
                g_ss.at[m, c], g_rs.at[m, c], {"pipe": below},
            )
            for c in range(chunks)
        ]
        for m in range(micro)
    ]

    flat_x = x_ref[...].reshape(micro * rows, width)
    for h in range(halves):
        if h == 1:
            wi_copy.wait_recv()
            wo_copy.start()
        pre = jnp.dot(flat_x, wi_halves[h][...], preferred_element_type=jnp.float32)
        for t in range(per):
            pre_send[h * per + t] = pre[:, t * quarter : (t + 1) * quarter]
    for copy in pre_copies:
        copy.start()

    def hidden_now(which):
        count = len(which)
        g_now = g_buf[which[0] : which[-1] + 1].reshape(count * rows, width)
        for h in range(halves):
            part = dot(g_now, wo_halves[h][...], LAST)
            for t in range(per):
                for i, m in enumerate(which):
                    hid_send[m, h * per + t] = part[i * rows : (i + 1) * rows, t * quarter : (t + 1) * quarter]
        for m in which:
            for copy in hid_copies[m]:
                copy.start()
        if pair:
            for m in which:
                gx_copies[m].start()

    def dpre_now(m):
        for copy in hid_copies[m]:
            copy.wait_recv()
        hidden = hid_send[m, me]
        for d in range(parts - 1):
            hidden = hidden + hid_recv[m, d]
        dpre_buf[m, me] = (hidden * slope_buf[m * rows : (m + 1) * rows, :]).astype(jnp.bfloat16)
        for copy in dp_copies[m]:
            copy.start()

    for copy in pre_copies:
        copy.wait_recv()
    mine = pre_send[me]
    for d in range(parts - 1):
        mine = mine + pre_recv[d]
    slope_buf[...] = silu_slope(mine)
    act_buf[me] = jax.nn.silu(mine).astype(jnp.bfloat16)
    for copy in act_copies:
        copy.start()

    if pair:
        wo_copy.wait_recv()
        x_copy.start()

    @pl.when(first)
    def _():
        hidden_now(list(range(micro)))
        for m in range(micro):
            dpre_now(m)

    for m in range(micro):
        @pl.when(section < pipes - 1)
        def _():
            for copy in g_copies[m]:
                copy.wait_recv()
            hidden_now([m])
            dpre_now(m)

        for copy in dp_copies[m]:
            copy.wait_recv()
        dpre_halves = [
            jnp.concatenate([dpre_buf[m, h * per + t] for t in range(per)], axis=1) for h in range(halves)
        ]
        for c in range(chunks):
            cols = pl.ds(c * step_w, step_w)
            total = g_buf[m, :, cols].astype(jnp.float32)
            for h in range(halves):
                total = total + dot(dpre_halves[h], wi_halves[h][cols, :], LAST)
            back_ref[m, :, cols] = total.astype(jnp.bfloat16)

            @pl.when(section > 0)
            def _():
                g_copies[m][c].start()

        if pair:
            dx_copies[m].start()
        if m == 0:
            for copy in act_copies:
                copy.wait_recv()
            if pair:
                actx_copy.start()

    sources = [(x_ref, g_buf, act_buf, dpre_buf)]
    if pair:
        x_copy.wait_recv()
        actx_copy.wait_recv()
        for m in range(micro):
            gx_copies[m].wait_recv()
            dx_copies[m].wait_recv()
        sources.append((x_other, g_other, act_other, dpre_other))
    ready = []
    for x_from, g_from, act_from, dpre_from in sources:
        act = jnp.concatenate([act_from[t] for t in range(per)], axis=1)
        dpre = jnp.concatenate(
            [dpre_from[:, t].reshape(micro * rows, quarter) for t in range(per)], axis=1
        )
        ready.append((x_from, g_from, act, dpre))

    for c in range(chunks):
        cols = pl.ds(c * step_w, step_w)
        grad_in, grad_out = 0.0, 0.0
        for x_from, g_from, act, dpre in ready:
            x_cols = x_from[:, :, cols].reshape(micro * rows, step_w)
            g_cols = g_from[:, :, cols].reshape(micro * rows, step_w)
            grad_in = grad_in + dot(x_cols, dpre, FIRST)
            grad_out = grad_out + dot(act, g_cols, FIRST)
        pin_ref[cols, :] = grad_in.astype(jnp.bfloat16)
        pout_ref[:, cols] = grad_out.astype(jnp.bfloat16)

    for copy in pre_copies + act_copies:
        copy.wait_send()
    if pair:
        for copy in [wi_copy, wo_copy, x_copy, actx_copy] + gx_copies + dx_copies:
            copy.wait_send()
    for m in range(micro):
        for copy in hid_copies[m] + dp_copies[m]:
            copy.wait_send()

        @pl.when(section > 0)
        def _():
            for copy in g_copies[m]:
                copy.wait_send()


def shards(acts, w_in, w_out, top_grad):
    pipes = lax.axis_size("pipe")
    parts = lax.axis_size("tensor")
    pair = lax.axis_size("dp") == 2 and parts % 2 == 0
    saved = acts[0]
    micro, rows, width = saved.shape
    if pair:
        out = pair_call(
            saved.reshape(micro * rows, width), w_in[0], w_out[0], top_grad.reshape(micro * rows, width)
        )
        return out[0].reshape(1, micro, rows, width), out[1][None], out[2][None]
    if pair:
        w_in_now, w_out_now = w_in[0], w_out[0]
    else:
        w_in_now = lax.all_gather(w_in[0], "dp", axis=1, tiled=True)
        w_out_now = lax.all_gather(w_out[0], "dp", axis=0, tiled=True)
    own = w_in_now.shape[1]
    per = parts // 2 if pair else parts
    quarter = own // per
    chunks = 4
    others = parts - 1
    bf, f32 = jnp.bfloat16, jnp.float32
    dma = pltpu.SemaphoreType.DMA
    vmem = pl.BlockSpec(memory_space=pltpu.VMEM)
    across = []
    if pair:
        across = [
            pltpu.VMEM((width, own), bf),
            pltpu.VMEM((own, width), bf),
            pltpu.VMEM((micro, rows, width), bf),
            pltpu.VMEM((micro, rows, width), bf),
            pltpu.VMEM((micro, per, rows, quarter), bf),
            pltpu.VMEM((per, micro * rows, quarter), bf),
            dma((4,)), dma((4,)),
            dma((micro,)), dma((micro,)), dma((micro,)), dma((micro,)),
        ]
    back, grad_in, grad_out = pl.pallas_call(
        functools.partial(chain, pipes, parts, pair, chunks),
        out_shape=(
            jax.ShapeDtypeStruct((micro, rows, width), bf),
            jax.ShapeDtypeStruct((width, own), bf),
            jax.ShapeDtypeStruct((own, width), bf),
        ),
        in_specs=[vmem] * 4,
        out_specs=(vmem,) * 3,
        scratch_shapes=[
            pltpu.VMEM((micro, rows, width), bf),
            pltpu.VMEM((parts, micro * rows, quarter), f32),
            pltpu.VMEM((others, micro * rows, quarter), f32),
            pltpu.VMEM((parts, micro * rows, quarter), bf),
            pltpu.VMEM((micro, parts, rows, quarter), f32),
            pltpu.VMEM((micro, others, rows, quarter), f32),
            pltpu.VMEM((micro, parts, rows, quarter), bf),
            pltpu.VMEM((micro * rows, quarter), f32),
            dma((others,)), dma((others,)), dma((others,)), dma((others,)),
            dma((micro, others)), dma((micro, others)),
            dma((micro, others)), dma((micro, others)),
            dma((micro, chunks)), dma((micro, chunks)),
            *across,
        ],
        compiler_params=pltpu.CompilerParams(
            collective_id=0, has_side_effects=True, vmem_limit_bytes=48 * 1024 * 1024
        ),
    )(saved, w_in_now, w_out_now, top_grad)
    if not pair:
        grad_in = lax.psum_scatter(grad_in, "dp", scatter_dimension=1, tiled=True)
        grad_out = lax.psum_scatter(grad_out, "dp", scatter_dimension=0, tiled=True)
    return back[None], grad_in[None], grad_out[None]


def solution(mesh):
    placed = (
        P("pipe", None, "dp", "tensor"),
        P("pipe", "tensor", "dp"),
        P("pipe", "dp", "tensor"),
        P(None, "dp", "tensor"),
    )
    return jax.shard_map(
        shards,
        mesh=mesh,
        in_specs=placed,
        out_specs=(
            P("pipe", None, "dp", "tensor"),
            P("pipe", "tensor", "dp"),
            P("pipe", "dp", "tensor"),
        ),
        check_vma=False,
    )
```

```python
import functools

import jax
import jax.numpy as jnp
from jax import lax
from jax.experimental import pallas as pl
from jax.experimental.pallas import tpu as pltpu
from jax.sharding import PartitionSpec as P

MESH = pl.DeviceIdType.MESH
LAST = (((1,), (1,)), ((), ()))
FIRST = (((0,), (0,)), ((), ()))
STEP = 16
LAG = 2
AHEAD = 3
BATCH = 32


def silu_slope(value):
    sig = jax.nn.sigmoid(value)
    return sig * (1.0 + value * (1.0 - sig))


def dot(left, right, dims):
    return lax.dot_general(left, right, dims, preferred_element_type=jnp.float32)


def mm(left, right):
    return jnp.dot(left, right, preferred_element_type=jnp.float32)


def remote(src, dst, send, recv, where):
    return pltpu.make_async_remote_copy(
        src_ref=src, dst_ref=dst, send_sem=send, recv_sem=recv,
        device_id=where, device_id_type=MESH,
    )


def paired(
    pipes, parts,
    x_hbm, wi_hbm, wo_hbm, top_hbm,
    back_ref, gin_ref, gout_ref,
    x_own, x_other, wi_own, wi_other, wo_own, wot, wit, g_own, g_other,
    pre_part, pre_recv, pre_full, slope, act, act_other, dpre, dpre_other,
    hid_own, hid_send, hid_recv, gin_acc, gout_acc,
    top_part, top_send, top_recv, far_part, far_recv, far_send, far_hid,
    top_ss, top_rs, far_ss, far_rs, over_ss, over_rs,
    pass_ss, pass_rs, on_ss, on_rs,
    load_sem, bulk_ss, bulk_rs, pre_ss, pre_rs, full_ss, full_rs,
    hid_ss, hid_rs, g_ss, g_rs, gx_ss, gx_rs, dx_ss, dx_rs,
):
    rows, width = x_own.shape
    own = wi_own.shape[1]
    count = rows // STEP
    share = rows // parts
    section = lax.axis_index("pipe")
    me = lax.axis_index("tensor")
    first = section == pipes - 1
    last = section == 0
    below = jnp.maximum(section - 1, 0)
    above = jnp.minimum(section + 1, pipes - 1)
    peers = [lax.rem(me + d, parts) for d in range(1, parts)]
    other = 1 - lax.axis_index("dp")
    partner = {"dp": other}

    barrier = pltpu.get_barrier_semaphore()
    for peer in peers:
        pl.semaphore_signal(barrier, inc=1, device_id={"tensor": peer}, device_id_type=MESH)
    for peer in [me] + peers:
        pl.semaphore_signal(
            barrier, inc=1, device_id={"dp": other, "tensor": peer}, device_id_type=MESH
        )

    @pl.when(section > 0)
    def _():
        pl.semaphore_signal(barrier, inc=1, device_id={"pipe": below}, device_id_type=MESH)

    @pl.when(section < pipes - 1)
    def _():
        pl.semaphore_signal(barrier, inc=1, device_id={"pipe": above}, device_id_type=MESH)

    loads = [
        pltpu.make_async_copy(src, dst, load_sem.at[i])
        for i, (src, dst) in enumerate([(x_hbm, x_own), (wi_hbm, wi_own), (wo_hbm, wo_own), (top_hbm, g_own)])
    ]
    for copy in loads[:3]:
        copy.start()

    @pl.when(first)
    def _():
        loads[3].start()

    beside = jnp.minimum(section, 1) + jnp.minimum(pipes - 1 - section, 1)
    pl.semaphore_wait(barrier, 2 * parts - 1 + beside)

    wi_copy = remote(wi_hbm, wi_other, bulk_ss.at[0], bulk_rs.at[0], partner)
    wo_copy = remote(wot.at[0], wot.at[1], bulk_ss.at[1], bulk_rs.at[1], partner)
    x_copy = remote(x_hbm, x_other, bulk_ss.at[2], bulk_rs.at[2], partner)
    my_share = pl.ds(pl.multiple_of(me * share, share), share)
    act_copy = remote(act.at[1, my_share], act_other.at[my_share], bulk_ss.at[3], bulk_rs.at[3], partner)
    pass_copies = [
        remote(act_other.at[my_share], act_other.at[my_share], pass_ss.at[d], pass_rs.at[d], {"tensor": peer})
        for d, peer in enumerate(peers)
    ]
    wi_copy.start()

    loads[2].wait()

    def turn_out(b, carry):
        cols = pl.ds(pl.multiple_of(b * 256, 256), 256)
        wot[0, cols, :] = wo_own[:, cols].T
        return carry

    lax.fori_loop(0, width // 256, turn_out, 0)

    @pl.when(section < pipes - 1)
    def _():
        wo_copy.start()
        x_copy.start()

    tile = 512
    tiles = width // tile
    group = tiles * STEP

    def rows_of(k):
        return pl.ds(pl.multiple_of(k * STEP, STEP), STEP)

    def g_copy(k):
        return remote(back_ref.at[rows_of(k)], g_own.at[rows_of(k)], g_ss.at[k], g_rs.at[k], {"pipe": below})

    def gx_copy(k):
        return remote(g_own.at[rows_of(k)], g_other.at[rows_of(k)], gx_ss.at[k], gx_rs.at[k], partner)

    def dx_copy(k):
        return remote(dpre.at[1, rows_of(k)], dpre_other.at[rows_of(k)], dx_ss.at[k], dx_rs.at[k], partner)

    def sends_dx(k):
        return (k >= count - tiles) | (lax.rem(k, parts) == me)

    def dx_start(k):
        @pl.when(sends_dx(k))
        def _():
            dx_copy(k).start()

    def on_copies(k):
        r = rows_of(k)
        return [
            remote(dpre_other.at[r], dpre_other.at[r], on_ss.at[k, d], on_rs.at[k, d], {"tensor": peer})
            for d, peer in enumerate(peers)
        ]

    def hid_copies(k):
        return [
            remote(hid_send.at[k], hid_recv.at[k, d], hid_ss.at[k, d], hid_rs.at[k, d], {"tensor": peer})
            for d, peer in enumerate(peers)
        ]

    per_batch = BATCH // STEP
    batch = BATCH
    piece = batch // parts
    batches = rows // batch

    def span(j, size):
        return pl.ds(pl.multiple_of(j * size, size), size)

    def top_copies():
        return [
            remote(top_send, top_recv.at[d], top_ss.at[d], top_rs.at[d], {"tensor": peer})
            for d, peer in enumerate(peers)
        ]

    def far_copies(j):
        return [
            remote(
                far_part.at[j, pl.ds(peer * piece, piece)], far_recv.at[j, d],
                far_ss.at[j, d], far_rs.at[j, d], {"tensor": peer},
            )
            for d, peer in enumerate(peers)
        ]

    def over_copies(j):
        return [
            remote(
                far_send.at[j], far_hid.at[j, d],
                over_ss.at[j, d], over_rs.at[j, d], {"dp": other, "tensor": peer},
            )
            for d, peer in enumerate([me] + peers)
        ]

    def send_top(j):
        for i in range(per_batch):
            gx_copy(per_batch * j + i).start()

    def far_start(j):
        for i in range(per_batch):
            gx_copy(per_batch * j + i).wait_recv()
        far_part[j] = mm(g_other[span(j, batch), :], wot[0])
        for copy in far_copies(j):
            copy.start()

    def far_sum(j):
        for copy in far_copies(j):
            copy.wait_recv()
        total = far_part[j, pl.ds(pl.multiple_of(me * piece, piece), piece), :]
        for d in range(parts - 1):
            total = total + far_recv[j, d]
        half = own // 2
        far_send[j] = jnp.concatenate([total[:, :half], total[:, half:]], axis=0).astype(jnp.bfloat16)
        for copy in over_copies(j):
            copy.start()

    def far_end(j):
        for copy in over_copies(j):
            copy.wait_recv()
        r = span(j, batch)
        near = top_part[r, :]
        for d in range(parts - 1):
            near = near + top_recv[d, r, :].astype(jnp.float32)
        total = g_own[r, :].astype(jnp.float32)
        slice_d = (near * slope[0, r, :]).astype(jnp.bfloat16)
        dpre[0, r, :] = slice_d
        total = total + mm(slice_d, wit[0])
        parts_now = []
        for t in range(parts):
            d = lax.rem(me - t + parts, parts)
            got = far_hid[j, d].astype(jnp.float32)
            parts_now.append(jnp.concatenate([got[:piece], got[piece:]], axis=1))
        slice_d = (jnp.concatenate(parts_now, axis=0) * slope[1, r, :]).astype(jnp.bfloat16)
        dpre[1, r, :] = slice_d
        total = total + mm(slice_d, wit[1])
        back_ref[r, :] = total.astype(jnp.bfloat16)
        for i in range(per_batch):
            g_copy(per_batch * j + i).start()
            dx_start(per_batch * j + i)

    def pre_copies(h):
        return [
            remote(
                pre_part.at[h, pl.ds(peer * share, share)], pre_recv.at[h, d],
                pre_ss.at[h, d], pre_rs.at[h, d], {"tensor": peer},
            )
            for d, peer in enumerate(peers)
        ]

    def full_copies(h):
        mine = pl.ds(me * share, share)
        return [
            remote(
                pre_full.at[h, mine], pre_full.at[h, mine],
                full_ss.at[h, d], full_rs.at[h, d], {"tensor": peer},
            )
            for d, peer in enumerate(peers)
        ]

    def turn_in(h, src):
        def body(b, carry):
            cols = pl.ds(pl.multiple_of(b * 256, 256), 256)
            wit[h, :, cols] = src[cols, :].T
            return carry

        lax.fori_loop(0, width // 256, body, 0)

    def pre_start(h, src):
        pre_part[h] = mm(x_own[...], src[...])
        for copy in pre_copies(h):
            copy.start()

    def pre_sum(h):
        for copy in pre_copies(h):
            copy.wait_recv()
        mine = pl.ds(pl.multiple_of(me * share, share), share)
        total = pre_part[h, mine, :]
        for d in range(parts - 1):
            total = total + pre_recv[h, d]
        pre_full[h, mine, :] = total
        for copy in full_copies(h):
            copy.start()

    def pre_end(h):
        for copy in full_copies(h):
            copy.wait_recv()
        value = pre_full[h]
        slope[h] = silu_slope(value)
        act[h] = jax.nn.silu(value).astype(jnp.bfloat16)

    @pl.when(first)
    def _():
        loads[3].wait()

        for j in range(AHEAD):
            send_top(j)
        near = mm(g_own[...], wot[0])
        top_part[...] = near
        top_send[...] = near.astype(jnp.bfloat16)
        for copy in top_copies():
            copy.start()

    loads[0].wait()
    loads[1].wait()
    pre_start(0, wi_own)
    turn_in(0, wi_own)
    pre_sum(0)
    pre_end(0)
    wi_copy.wait_recv()
    pre_start(1, wi_other)
    turn_in(1, wi_other)
    pre_sum(1)

    @pl.when(first)
    def _():
        far_start(0)
        send_top(AHEAD)
        for copy in top_copies():
            copy.wait_recv()

    pre_end(1)

    @pl.when(first)
    def _():
        def steps(j, carry):
            @pl.when(j < batches)
            def _():
                far_start(j)

                @pl.when(j + AHEAD < batches)
                def _():
                    send_top(j + AHEAD)

            @pl.when(j <= batches)
            def _():
                far_sum(j - 1)

            @pl.when(j >= 2)
            def _():
                far_end(j - 2)

            return carry

        lax.fori_loop(1, batches + 2, steps, 0)
        x_copy.start()
        act_copy.start()

    def hidden_now(k):
        g_copy(k).wait_recv()
        gx_copy(k).start()
        g_now = g_own[rows_of(k), :]
        for h in range(2):
            part = mm(g_now, wot[h])
            hid_own[k, h] = part
            hid_send[k, h] = part.astype(jnp.bfloat16)
        for copy in hid_copies(k):
            copy.start()

    def back_now(k):
        for copy in hid_copies(k):
            copy.wait_recv()
        total = g_own[rows_of(k), :].astype(jnp.float32)
        for h in range(2):
            hidden = hid_own[k, h]
            for d in range(parts - 1):
                hidden = hidden + hid_recv[k, d, h].astype(jnp.float32)
            slice_d = (hidden * slope[h, rows_of(k), :]).astype(jnp.bfloat16)
            dpre[h, rows_of(k), :] = slice_d
            total = total + mm(slice_d, wit[h])
        back_ref[rows_of(k), :] = total.astype(jnp.bfloat16)

        @pl.when(section > 0)
        def _():
            g_copy(k).start()

        dx_start(k)

    def own_tile(r, c, start):
        cols = span(c, tile)
        part_in = dot(x_own[r, cols], dpre[0, r, :], FIRST)
        part_out = dot(act[0, r, :], g_own[r, cols], FIRST)
        if start:
            gin_acc[cols, :] = part_in
            gout_acc[:, cols] = part_out
        else:
            gin_acc[cols, :] += part_in
            gout_acc[:, cols] += part_out

    def chain(k, carry):
        @pl.when(k < count)
        def _():
            hidden_now(k)

        done = k - LAG

        @pl.when(done >= 0)
        def _():
            back_now(done)

        @pl.when((done >= tiles) & (done < 2 * tiles))
        def _():
            own_tile(pl.ds(0, group), lax.rem(done, tiles), True)

        @pl.when(done >= 2 * tiles)
        def _():
            own_tile(span(done // tiles - 1, group), lax.rem(done, tiles), False)

        return carry

    @pl.when(section < pipes - 1)
    def _():
        act_copy.start()
        wo_copy.wait_recv()
        lax.fori_loop(0, count + LAG, chain, 0)

    @pl.when(first)
    def _():
        def all_own(c, carry):
            own_tile(pl.ds(0, rows - group), c, True)
            return carry

        lax.fori_loop(0, tiles, all_own, 0)

    act_copy.wait_recv()
    for copy in pass_copies:
        copy.start()

    def move_on(i, carry):
        k = i * parts + me
        dx_copy(k).wait_recv()
        for copy in on_copies(k):
            copy.start()
        return carry

    lax.fori_loop(0, (count - tiles) // parts, move_on, 0)
    for copy in pass_copies:
        copy.wait_recv()

    early, late = pl.ds(0, rows - group), pl.ds(rows - group, group)

    def wait_gx(k, carry):
        gx_copy(k).wait_recv()
        return carry

    def wait_dx(k, carry):
        dx_copy(k).wait_recv()
        return carry

    @pl.when(section < pipes - 1)
    def _():
        lax.fori_loop(0, count - tiles, wait_gx, 0)

    def early_tile(c, carry):
        cols = span(c, tile)
        gout_acc[:, cols] += dot(act_other[early, :], g_other[early, cols], FIRST)
        return carry

    lax.fori_loop(0, tiles, early_tile, 0)
    x_copy.wait_recv()

    def wait_on(k, carry):
        source = lax.rem(k, parts)

        @pl.when(source != me)
        def _():
            d = lax.rem(me - source + parts, parts) - 1
            r = rows_of(k)
            remote(dpre_other.at[r], dpre_other.at[r], on_ss.at[k, d], on_rs.at[k, d], partner).wait_recv()

        return carry

    lax.fori_loop(0, count - tiles, wait_on, 0)

    def early_in(c, carry):
        cols = span(c, tile)
        gin_acc[cols, :] += dot(x_other[early, cols], dpre_other[early, :], FIRST)
        return carry

    lax.fori_loop(0, tiles, early_in, 0)

    @pl.when(section < pipes - 1)
    def _():
        lax.fori_loop(count - tiles, count, wait_gx, 0)

    lax.fori_loop(count - tiles, count, wait_dx, 0)

    def end_tile(c, carry):
        cols = span(c, tile)
        part_in = dot(x_own[late, cols], dpre[0, late, :], FIRST) + dot(x_other[late, cols], dpre_other[late, :], FIRST)
        part_out = dot(act[0, late, :], g_own[late, cols], FIRST) + dot(act_other[late, :], g_other[late, cols], FIRST)
        gin_ref[cols, :] = (gin_acc[cols, :] + part_in).astype(jnp.bfloat16)
        gout_ref[:, cols] = (gout_acc[:, cols] + part_out).astype(jnp.bfloat16)
        return carry

    lax.fori_loop(0, tiles, end_tile, 0)

    for copy in [wi_copy, x_copy, act_copy] + pass_copies:
        copy.wait_send()

    @pl.when(section < pipes - 1)
    def _():
        wo_copy.wait_send()

    @pl.when(first)
    def _():
        for copy in top_copies():
            copy.wait_send()

        def drain_far(j, carry):
            for copy in far_copies(j) + over_copies(j):
                copy.wait_send()
            return carry

        lax.fori_loop(0, batches, drain_far, 0)

    for h in range(2):
        for copy in pre_copies(h) + full_copies(h):
            copy.wait_send()

    def drain(k, carry):
        gx_copy(k).wait_send()

        @pl.when(sends_dx(k))
        def _():
            dx_copy(k).wait_send()

        @pl.when((k < count - tiles) & (lax.rem(k, parts) == me))
        def _():
            for copy in on_copies(k):
                copy.wait_send()

        @pl.when(section < pipes - 1)
        def _():
            for copy in hid_copies(k):
                copy.wait_send()

        @pl.when(section > 0)
        def _():
            g_copy(k).wait_send()

        return carry

    lax.fori_loop(0, count, drain, 0)


def flush(*refs):
    count = (len(refs) - 1) // 2
    sems = refs[-1]
    copies = []
    for i in range(count):
        src, dst = refs[i], refs[count + i]
        half = src.shape[0] // 2
        for j in range(2):
            r = pl.ds(j * half, half)
            copies.append(pltpu.make_async_copy(src.at[r], dst.at[r], sems.at[i, j]))
    for copy in copies:
        copy.start()
    for copy in copies:
        copy.wait()


def written(arrays):
    return pl.pallas_call(
        flush,
        out_shape=tuple(jax.ShapeDtypeStruct(a.shape, a.dtype) for a in arrays),
        in_specs=[pl.BlockSpec(memory_space=pltpu.VMEM)] * len(arrays),
        out_specs=tuple(pl.BlockSpec(memory_space=pl.ANY) for _ in arrays),
        scratch_shapes=[pltpu.SemaphoreType.DMA((len(arrays), 2))],
        compiler_params=pltpu.CompilerParams(vmem_limit_bytes=1024 * 1024),
    )(*arrays)


def pair_call(saved, w_in_now, w_out_now, top):
    pipes = lax.axis_size("pipe")
    parts = lax.axis_size("tensor")
    rows, width = saved.shape
    own = w_in_now.shape[1]
    count = rows // STEP
    share = rows // parts
    batches = rows // BATCH
    piece = BATCH // parts
    others = parts - 1
    bf, f32 = jnp.bfloat16, jnp.float32
    dma = pltpu.SemaphoreType.DMA
    vmem = pl.BlockSpec(memory_space=pltpu.VMEM)
    anywhere = pl.BlockSpec(memory_space=pl.ANY)
    return pl.pallas_call(
        functools.partial(paired, pipes, parts),
        out_shape=(
            jax.ShapeDtypeStruct((rows, width), bf),
            jax.ShapeDtypeStruct((width, own), bf),
            jax.ShapeDtypeStruct((own, width), bf),
        ),
        in_specs=[anywhere] * 4,
        out_specs=(vmem,) * 3,
        scratch_shapes=[
            pltpu.VMEM((rows, width), bf),
            pltpu.VMEM((rows, width), bf),
            pltpu.VMEM((width, own), bf),
            pltpu.VMEM((width, own), bf),
            pltpu.VMEM((own, width), bf),
            pltpu.VMEM((2, width, own), bf),
            pltpu.VMEM((2, own, width), bf),
            pltpu.VMEM((rows, width), bf),
            pltpu.VMEM((rows, width), bf),
            pltpu.VMEM((2, rows, own), f32),
            pltpu.VMEM((2, others, share, own), f32),
            pltpu.VMEM((2, rows, own), f32),
            pltpu.VMEM((2, rows, own), f32),
            pltpu.VMEM((2, rows, own), bf),
            pltpu.VMEM((rows, own), bf),
            pltpu.VMEM((2, rows, own), bf),
            pltpu.VMEM((rows, own), bf),
            pltpu.VMEM((count, 2, STEP, own), f32),
            pltpu.VMEM((count, 2, STEP, own), bf),
            pltpu.VMEM((count, others, 2, STEP, own), bf),
            pltpu.VMEM((width, own), f32),
            pltpu.VMEM((own, width), f32),
            pltpu.VMEM((rows, own), f32),
            pltpu.VMEM((rows, own), bf),
            pltpu.VMEM((others, rows, own), bf),
            pltpu.VMEM((batches, BATCH, own), f32),
            pltpu.VMEM((batches, others, piece, own), f32),
            pltpu.VMEM((batches, 2 * piece, own // 2), bf),
            pltpu.VMEM((batches, parts, 2 * piece, own // 2), bf),
            dma((others,)), dma((others,)),
            dma((batches, others)), dma((batches, others)),
            dma((batches, parts)), dma((batches, parts)),
            dma((others,)), dma((others,)), dma((count, others)), dma((count, others)),
            dma((4,)), dma((4,)), dma((4,)),
            dma((2, others)), dma((2, others)), dma((2, others)), dma((2, others)),
            dma((count, others)), dma((count, others)),
            dma((count,)), dma((count,)), dma((count,)), dma((count,)), dma((count,)), dma((count,)),
        ],
        compiler_params=pltpu.CompilerParams(
            collective_id=0, has_side_effects=True, vmem_limit_bytes=50 * 1024 * 1024
        ),
    )(saved, w_in_now, w_out_now, top)


def chain(
    pipes, parts, pair, chunks,
    x_ref, wi_ref, wo_ref, top_ref,
    back_ref, pin_ref, pout_ref,
    g_buf, pre_send, pre_recv, act_buf, hid_send, hid_recv, dpre_buf, slope_buf,
    pre_ss, pre_rs, act_ss, act_rs, hid_ss, hid_rs, dp_ss, dp_rs, g_ss, g_rs,
    *across,
):
    micro, rows, width = x_ref.shape
    own = wi_ref.shape[1]
    halves = 2 if pair else 1
    per = parts // halves
    quarter = own // per
    step_w = width // chunks
    section = lax.axis_index("pipe")
    me = lax.axis_index("tensor")
    first = section == pipes - 1
    below = jnp.maximum(section - 1, 0)
    above = jnp.minimum(section + 1, pipes - 1)
    peers = [lax.rem(me + d, parts) for d in range(1, parts)]

    barrier = pltpu.get_barrier_semaphore()
    for peer in peers:
        pl.semaphore_signal(barrier, inc=1, device_id={"tensor": peer}, device_id_type=MESH)
    if pair:
        partner = {"dp": 1 - lax.axis_index("dp")}
        pl.semaphore_signal(barrier, inc=1, device_id=partner, device_id_type=MESH)

    @pl.when(section > 0)
    def _():
        pl.semaphore_signal(barrier, inc=1, device_id={"pipe": below}, device_id_type=MESH)

    @pl.when(section < pipes - 1)
    def _():
        pl.semaphore_signal(barrier, inc=1, device_id={"pipe": above}, device_id_type=MESH)

    beside = jnp.minimum(section, 1) + jnp.minimum(pipes - 1 - section, 1)
    pl.semaphore_wait(barrier, parts - 1 + halves - 1 + beside)

    def remote(src, dst, send, recv, where):
        return pltpu.make_async_remote_copy(
            src_ref=src, dst_ref=dst, send_sem=send, recv_sem=recv,
            device_id=where, device_id_type=MESH,
        )

    wi_halves, wo_halves = [wi_ref], [wo_ref]
    if pair:
        wi_other, wo_other, x_other, g_other, dpre_other, act_other, one_ss, one_rs, gx_ss, gx_rs, dx_ss, dx_rs = across
        wi_halves.append(wi_other)
        wo_halves.append(wo_other)
        wi_copy = remote(wi_ref, wi_other, one_ss.at[0], one_rs.at[0], partner)
        wo_copy = remote(wo_ref, wo_other, one_ss.at[1], one_rs.at[1], partner)
        x_copy = remote(x_ref, x_other, one_ss.at[2], one_rs.at[2], partner)
        actx_copy = remote(act_buf.at[pl.ds(per, per)], act_other, one_ss.at[3], one_rs.at[3], partner)
        gx_copies = [remote(g_buf.at[m], g_other.at[m], gx_ss.at[m], gx_rs.at[m], partner) for m in range(micro)]
        dx_copies = [
            remote(dpre_buf.at[m, pl.ds(per, per)], dpre_other.at[m], dx_ss.at[m], dx_rs.at[m], partner)
            for m in range(micro)
        ]
        wi_copy.start()

    @pl.when(first)
    def _():
        g_buf[...] = top_ref[...]

    pre_copies = [
        remote(pre_send.at[peer], pre_recv.at[d], pre_ss.at[d], pre_rs.at[d], {"tensor": peer})
        for d, peer in enumerate(peers)
    ]
    hid_copies = [
        [
            remote(hid_send.at[m, peer], hid_recv.at[m, d], hid_ss.at[m, d], hid_rs.at[m, d], {"tensor": peer})
            for d, peer in enumerate(peers)
        ]
        for m in range(micro)
    ]
    dp_copies = [
        [
            remote(dpre_buf.at[m, me], dpre_buf.at[m, me], dp_ss.at[m, d], dp_rs.at[m, d], {"tensor": peer})
            for d, peer in enumerate(peers)
        ]
        for m in range(micro)
    ]
    act_copies = [
        remote(act_buf.at[me], act_buf.at[me], act_ss.at[d], act_rs.at[d], {"tensor": peer})
        for d, peer in enumerate(peers)
    ]
    g_copies = [
        [
            remote(
                back_ref.at[m, :, pl.ds(c * step_w, step_w)], g_buf.at[m, :, pl.ds(c * step_w, step_w)],
                g_ss.at[m, c], g_rs.at[m, c], {"pipe": below},
            )
            for c in range(chunks)
        ]
        for m in range(micro)
    ]

    flat_x = x_ref[...].reshape(micro * rows, width)
    for h in range(halves):
        if h == 1:
            wi_copy.wait_recv()
            wo_copy.start()
        pre = jnp.dot(flat_x, wi_halves[h][...], preferred_element_type=jnp.float32)
        for t in range(per):
            pre_send[h * per + t] = pre[:, t * quarter : (t + 1) * quarter]
    for copy in pre_copies:
        copy.start()

    def hidden_now(which):
        count = len(which)
        g_now = g_buf[which[0] : which[-1] + 1].reshape(count * rows, width)
        for h in range(halves):
            part = dot(g_now, wo_halves[h][...], LAST)
            for t in range(per):
                for i, m in enumerate(which):
                    hid_send[m, h * per + t] = part[i * rows : (i + 1) * rows, t * quarter : (t + 1) * quarter]
        for m in which:
            for copy in hid_copies[m]:
                copy.start()
        if pair:
            for m in which:
                gx_copies[m].start()

    def dpre_now(m):
        for copy in hid_copies[m]:
            copy.wait_recv()
        hidden = hid_send[m, me]
        for d in range(parts - 1):
            hidden = hidden + hid_recv[m, d]
        dpre_buf[m, me] = (hidden * slope_buf[m * rows : (m + 1) * rows, :]).astype(jnp.bfloat16)
        for copy in dp_copies[m]:
            copy.start()

    for copy in pre_copies:
        copy.wait_recv()
    mine = pre_send[me]
    for d in range(parts - 1):
        mine = mine + pre_recv[d]
    slope_buf[...] = silu_slope(mine)
    act_buf[me] = jax.nn.silu(mine).astype(jnp.bfloat16)
    for copy in act_copies:
        copy.start()

    if pair:
        wo_copy.wait_recv()
        x_copy.start()

    @pl.when(first)
    def _():
        hidden_now(list(range(micro)))
        for m in range(micro):
            dpre_now(m)

    for m in range(micro):
        @pl.when(section < pipes - 1)
        def _():
            for copy in g_copies[m]:
                copy.wait_recv()
            hidden_now([m])
            dpre_now(m)

        for copy in dp_copies[m]:
            copy.wait_recv()
        dpre_halves = [
            jnp.concatenate([dpre_buf[m, h * per + t] for t in range(per)], axis=1) for h in range(halves)
        ]
        for c in range(chunks):
            cols = pl.ds(c * step_w, step_w)
            total = g_buf[m, :, cols].astype(jnp.float32)
            for h in range(halves):
                total = total + dot(dpre_halves[h], wi_halves[h][cols, :], LAST)
            back_ref[m, :, cols] = total.astype(jnp.bfloat16)

            @pl.when(section > 0)
            def _():
                g_copies[m][c].start()

        if pair:
            dx_copies[m].start()
        if m == 0:
            for copy in act_copies:
                copy.wait_recv()
            if pair:
                actx_copy.start()

    sources = [(x_ref, g_buf, act_buf, dpre_buf)]
    if pair:
        x_copy.wait_recv()
        actx_copy.wait_recv()
        for m in range(micro):
            gx_copies[m].wait_recv()
            dx_copies[m].wait_recv()
        sources.append((x_other, g_other, act_other, dpre_other))
    ready = []
    for x_from, g_from, act_from, dpre_from in sources:
        act = jnp.concatenate([act_from[t] for t in range(per)], axis=1)
        dpre = jnp.concatenate(
            [dpre_from[:, t].reshape(micro * rows, quarter) for t in range(per)], axis=1
        )
        ready.append((x_from, g_from, act, dpre))

    for c in range(chunks):
        cols = pl.ds(c * step_w, step_w)
        grad_in, grad_out = 0.0, 0.0
        for x_from, g_from, act, dpre in ready:
            x_cols = x_from[:, :, cols].reshape(micro * rows, step_w)
            g_cols = g_from[:, :, cols].reshape(micro * rows, step_w)
            grad_in = grad_in + dot(x_cols, dpre, FIRST)
            grad_out = grad_out + dot(act, g_cols, FIRST)
        pin_ref[cols, :] = grad_in.astype(jnp.bfloat16)
        pout_ref[:, cols] = grad_out.astype(jnp.bfloat16)

    for copy in pre_copies + act_copies:
        copy.wait_send()
    if pair:
        for copy in [wi_copy, wo_copy, x_copy, actx_copy] + gx_copies + dx_copies:
            copy.wait_send()
    for m in range(micro):
        for copy in hid_copies[m] + dp_copies[m]:
            copy.wait_send()

        @pl.when(section > 0)
        def _():
            for copy in g_copies[m]:
                copy.wait_send()


def shards(acts, w_in, w_out, top_grad):
    pipes = lax.axis_size("pipe")
    parts = lax.axis_size("tensor")
    pair = lax.axis_size("dp") == 2 and parts % 2 == 0
    saved = acts[0]
    micro, rows, width = saved.shape
    if pair:
        out = written(pair_call(
            saved.reshape(micro * rows, width), w_in[0], w_out[0], top_grad.reshape(micro * rows, width)
        ))
        return out[0].reshape(1, micro, rows, width), out[1][None], out[2][None]
    if pair:
        w_in_now, w_out_now = w_in[0], w_out[0]
    else:
        w_in_now = lax.all_gather(w_in[0], "dp", axis=1, tiled=True)
        w_out_now = lax.all_gather(w_out[0], "dp", axis=0, tiled=True)
    own = w_in_now.shape[1]
    per = parts // 2 if pair else parts
    quarter = own // per
    chunks = 4
    others = parts - 1
    bf, f32 = jnp.bfloat16, jnp.float32
    dma = pltpu.SemaphoreType.DMA
    vmem = pl.BlockSpec(memory_space=pltpu.VMEM)
    across = []
    if pair:
        across = [
            pltpu.VMEM((width, own), bf),
            pltpu.VMEM((own, width), bf),
            pltpu.VMEM((micro, rows, width), bf),
            pltpu.VMEM((micro, rows, width), bf),
            pltpu.VMEM((micro, per, rows, quarter), bf),
            pltpu.VMEM((per, micro * rows, quarter), bf),
            dma((4,)), dma((4,)),
            dma((micro,)), dma((micro,)), dma((micro,)), dma((micro,)),
        ]
    back, grad_in, grad_out = pl.pallas_call(
        functools.partial(chain, pipes, parts, pair, chunks),
        out_shape=(
            jax.ShapeDtypeStruct((micro, rows, width), bf),
            jax.ShapeDtypeStruct((width, own), bf),
            jax.ShapeDtypeStruct((own, width), bf),
        ),
        in_specs=[vmem] * 4,
        out_specs=(vmem,) * 3,
        scratch_shapes=[
            pltpu.VMEM((micro, rows, width), bf),
            pltpu.VMEM((parts, micro * rows, quarter), f32),
            pltpu.VMEM((others, micro * rows, quarter), f32),
            pltpu.VMEM((parts, micro * rows, quarter), bf),
            pltpu.VMEM((micro, parts, rows, quarter), f32),
            pltpu.VMEM((micro, others, rows, quarter), f32),
            pltpu.VMEM((micro, parts, rows, quarter), bf),
            pltpu.VMEM((micro * rows, quarter), f32),
            dma((others,)), dma((others,)), dma((others,)), dma((others,)),
            dma((micro, others)), dma((micro, others)),
            dma((micro, others)), dma((micro, others)),
            dma((micro, chunks)), dma((micro, chunks)),
            *across,
        ],
        compiler_params=pltpu.CompilerParams(
            collective_id=0, has_side_effects=True, vmem_limit_bytes=48 * 1024 * 1024
        ),
    )(saved, w_in_now, w_out_now, top_grad)
    if not pair:
        grad_in = lax.psum_scatter(grad_in, "dp", scatter_dimension=1, tiled=True)
        grad_out = lax.psum_scatter(grad_out, "dp", scatter_dimension=0, tiled=True)
    return back[None], grad_in[None], grad_out[None]


def solution(mesh):
    placed = (
        P("pipe", None, "dp", "tensor"),
        P("pipe", "tensor", "dp"),
        P("pipe", "dp", "tensor"),
        P(None, "dp", "tensor"),
    )
    return jax.shard_map(
        shards,
        mesh=mesh,
        in_specs=placed,
        out_specs=(
            P("pipe", None, "dp", "tensor"),
            P("pipe", "tensor", "dp"),
            P("pipe", "dp", "tensor"),
        ),
        check_vma=False,
    )
```

```python
import functools

import jax
import jax.numpy as jnp
from jax import lax
from jax.experimental import pallas as pl
from jax.experimental.pallas import tpu as pltpu
from jax.sharding import PartitionSpec as P

MESH = pl.DeviceIdType.MESH
LAST = (((1,), (1,)), ((), ()))
FIRST = (((0,), (0,)), ((), ()))
STEP = 16
LAG = 2
AHEAD = 3
BATCH = 32


def silu_slope(value):
    sig = jax.nn.sigmoid(value)
    return sig * (1.0 + value * (1.0 - sig))


def dot(left, right, dims):
    return lax.dot_general(left, right, dims, preferred_element_type=jnp.float32)


def mm(left, right):
    return jnp.dot(left, right, preferred_element_type=jnp.float32)


def remote(src, dst, send, recv, where):
    return pltpu.make_async_remote_copy(
        src_ref=src, dst_ref=dst, send_sem=send, recv_sem=recv,
        device_id=where, device_id_type=MESH,
    )


def paired(
    pipes, parts,
    x_hbm, wi_hbm, wo_hbm, top_hbm,
    back_ref, gin_ref, gout_ref,
    x_own, x_other, wi_own, wi_other, wo_own, wot, wit, g_own, g_other,
    pre_part, pre_recv, pre_full, slope, act, act_other, dpre, dpre_other,
    hid_own, hid_send, hid_recv, gin_acc, gout_acc,
    top_part, top_send, top_recv, far_part, far_recv, far_send, far_hid,
    top_ss, top_rs, far_ss, far_rs, over_ss, over_rs,
    pass_ss, pass_rs, on_ss, on_rs,
    load_sem, bulk_ss, bulk_rs, pre_ss, pre_rs, full_ss, full_rs,
    hid_ss, hid_rs, g_ss, g_rs, gx_ss, gx_rs, dx_ss, dx_rs,
):
    rows, width = x_own.shape
    own = wi_own.shape[1]
    count = rows // STEP
    share = rows // parts
    section = lax.axis_index("pipe")
    me = lax.axis_index("tensor")
    first = section == pipes - 1
    last = section == 0
    below = jnp.maximum(section - 1, 0)
    above = jnp.minimum(section + 1, pipes - 1)
    peers = [lax.rem(me + d, parts) for d in range(1, parts)]
    other = 1 - lax.axis_index("dp")
    partner = {"dp": other}

    barrier = pltpu.get_barrier_semaphore()
    for peer in peers:
        pl.semaphore_signal(barrier, inc=1, device_id={"tensor": peer}, device_id_type=MESH)
    for peer in [me] + peers:
        pl.semaphore_signal(
            barrier, inc=1, device_id={"dp": other, "tensor": peer}, device_id_type=MESH
        )

    @pl.when(section > 0)
    def _():
        pl.semaphore_signal(barrier, inc=1, device_id={"pipe": below}, device_id_type=MESH)

    @pl.when(section < pipes - 1)
    def _():
        pl.semaphore_signal(barrier, inc=1, device_id={"pipe": above}, device_id_type=MESH)

    loads = [
        pltpu.make_async_copy(src, dst, load_sem.at[i])
        for i, (src, dst) in enumerate([(x_hbm, x_own), (wi_hbm, wi_own), (wo_hbm, wo_own), (top_hbm, g_own)])
    ]
    for copy in loads[:3]:
        copy.start()

    @pl.when(first)
    def _():
        loads[3].start()

    beside = jnp.minimum(section, 1) + jnp.minimum(pipes - 1 - section, 1)
    pl.semaphore_wait(barrier, 2 * parts - 1 + beside)

    wi_copy = remote(wi_hbm, wi_other, bulk_ss.at[0], bulk_rs.at[0], partner)
    wo_copy = remote(wot.at[0], wot.at[1], bulk_ss.at[1], bulk_rs.at[1], partner)
    x_copy = remote(x_hbm, x_other, bulk_ss.at[2], bulk_rs.at[2], partner)
    my_share = pl.ds(pl.multiple_of(me * share, share), share)
    act_copy = remote(act.at[1, my_share], act_other.at[my_share], bulk_ss.at[3], bulk_rs.at[3], partner)
    pass_copies = [
        remote(act_other.at[my_share], act_other.at[my_share], pass_ss.at[d], pass_rs.at[d], {"tensor": peer})
        for d, peer in enumerate(peers)
    ]
    wi_copy.start()

    loads[2].wait()

    def turn_out(b, carry):
        cols = pl.ds(pl.multiple_of(b * 256, 256), 256)
        wot[0, cols, :] = wo_own[:, cols].T
        return carry

    lax.fori_loop(0, width // 256, turn_out, 0)

    @pl.when(section < pipes - 1)
    def _():
        wo_copy.start()
        x_copy.start()

    tile = 512
    tiles = width // tile
    group = tiles * STEP

    def rows_of(k):
        return pl.ds(pl.multiple_of(k * STEP, STEP), STEP)

    def g_copy(k):
        return remote(back_ref.at[rows_of(k)], g_own.at[rows_of(k)], g_ss.at[k], g_rs.at[k], {"pipe": below})

    def gx_copy(k):
        return remote(g_own.at[rows_of(k)], g_other.at[rows_of(k)], gx_ss.at[k], gx_rs.at[k], partner)

    def dx_copy(k):
        return remote(dpre.at[1, rows_of(k)], dpre_other.at[rows_of(k)], dx_ss.at[k], dx_rs.at[k], partner)

    def sends_dx(k):
        return (k >= count - tiles) | (lax.rem(k, parts) == me)

    def dx_start(k):
        @pl.when(sends_dx(k))
        def _():
            dx_copy(k).start()

    def on_copies(k):
        r = rows_of(k)
        return [
            remote(dpre_other.at[r], dpre_other.at[r], on_ss.at[k, d], on_rs.at[k, d], {"tensor": peer})
            for d, peer in enumerate(peers)
        ]

    def hid_copies(k):
        return [
            remote(hid_send.at[k], hid_recv.at[k, d], hid_ss.at[k, d], hid_rs.at[k, d], {"tensor": peer})
            for d, peer in enumerate(peers)
        ]

    per_batch = BATCH // STEP
    batch = BATCH
    piece = batch // parts
    batches = rows // batch

    def span(j, size):
        return pl.ds(pl.multiple_of(j * size, size), size)

    def top_copies():
        return [
            remote(top_send, top_recv.at[d], top_ss.at[d], top_rs.at[d], {"tensor": peer})
            for d, peer in enumerate(peers)
        ]

    def far_copies(j):
        return [
            remote(
                far_part.at[j, pl.ds(peer * piece, piece)], far_recv.at[j, d],
                far_ss.at[j, d], far_rs.at[j, d], {"tensor": peer},
            )
            for d, peer in enumerate(peers)
        ]

    def over_copies(j):
        return [
            remote(
                far_send.at[j], far_hid.at[j, d],
                over_ss.at[j, d], over_rs.at[j, d], {"dp": other, "tensor": peer},
            )
            for d, peer in enumerate([me] + peers)
        ]

    def send_top(j):
        for i in range(per_batch):
            gx_copy(per_batch * j + i).start()

    def far_start(j):
        for i in range(per_batch):
            gx_copy(per_batch * j + i).wait_recv()
        far_part[j] = mm(g_other[span(j, batch), :], wot[0])
        for copy in far_copies(j):
            copy.start()

    def far_sum(j):
        for copy in far_copies(j):
            copy.wait_recv()
        total = far_part[j, pl.ds(pl.multiple_of(me * piece, piece), piece), :]
        for d in range(parts - 1):
            total = total + far_recv[j, d]
        half = own // 2
        far_send[j] = jnp.concatenate([total[:, :half], total[:, half:]], axis=0).astype(jnp.bfloat16)
        for copy in over_copies(j):
            copy.start()

    def far_end(j):
        for copy in over_copies(j):
            copy.wait_recv()
        r = span(j, batch)
        near = top_part[r, :]
        for d in range(parts - 1):
            near = near + top_recv[d, r, :].astype(jnp.float32)
        total = g_own[r, :].astype(jnp.float32)
        slice_d = (near * slope[0, r, :]).astype(jnp.bfloat16)
        dpre[0, r, :] = slice_d
        total = total + mm(slice_d, wit[0])
        parts_now = []
        for t in range(parts):
            d = lax.rem(me - t + parts, parts)
            got = far_hid[j, d].astype(jnp.float32)
            parts_now.append(jnp.concatenate([got[:piece], got[piece:]], axis=1))
        slice_d = (jnp.concatenate(parts_now, axis=0) * slope[1, r, :]).astype(jnp.bfloat16)
        dpre[1, r, :] = slice_d
        total = total + mm(slice_d, wit[1])
        back_ref[r, :] = total.astype(jnp.bfloat16)
        for i in range(per_batch):
            g_copy(per_batch * j + i).start()
            dx_start(per_batch * j + i)

    def pre_copies(h):
        return [
            remote(
                pre_part.at[h, pl.ds(peer * share, share)], pre_recv.at[h, d],
                pre_ss.at[h, d], pre_rs.at[h, d], {"tensor": peer},
            )
            for d, peer in enumerate(peers)
        ]

    def full_copies(h):
        mine = pl.ds(me * share, share)
        return [
            remote(
                pre_full.at[h, mine], pre_full.at[h, mine],
                full_ss.at[h, d], full_rs.at[h, d], {"tensor": peer},
            )
            for d, peer in enumerate(peers)
        ]

    def turn_in(h, src):
        def body(b, carry):
            cols = pl.ds(pl.multiple_of(b * 256, 256), 256)
            wit[h, :, cols] = src[cols, :].T
            return carry

        lax.fori_loop(0, width // 256, body, 0)

    def pre_start(h, src):
        pre_part[h] = mm(x_own[...], src[...])
        for copy in pre_copies(h):
            copy.start()

    def pre_sum(h):
        for copy in pre_copies(h):
            copy.wait_recv()
        mine = pl.ds(pl.multiple_of(me * share, share), share)
        total = pre_part[h, mine, :]
        for d in range(parts - 1):
            total = total + pre_recv[h, d]
        pre_full[h, mine, :] = total
        for copy in full_copies(h):
            copy.start()

    def pre_end(h):
        for copy in full_copies(h):
            copy.wait_recv()
        value = pre_full[h]
        slope[h] = silu_slope(value)
        act[h] = jax.nn.silu(value).astype(jnp.bfloat16)

    @pl.when(first)
    def _():
        loads[3].wait()

        for j in range(AHEAD):
            send_top(j)
        near = mm(g_own[...], wot[0])
        top_part[...] = near
        top_send[...] = near.astype(jnp.bfloat16)
        for copy in top_copies():
            copy.start()

    loads[0].wait()
    loads[1].wait()
    pre_start(0, wi_own)
    turn_in(0, wi_own)
    pre_sum(0)
    pre_end(0)
    wi_copy.wait_recv()
    pre_start(1, wi_other)
    turn_in(1, wi_other)
    pre_sum(1)

    @pl.when(first)
    def _():
        far_start(0)
        send_top(AHEAD)
        for copy in top_copies():
            copy.wait_recv()

    pre_end(1)

    @pl.when(first)
    def _():
        def steps(j, carry):
            @pl.when(j < batches)
            def _():
                far_start(j)

                @pl.when(j + AHEAD < batches)
                def _():
                    send_top(j + AHEAD)

            @pl.when(j <= batches)
            def _():
                far_sum(j - 1)

            @pl.when(j >= 2)
            def _():
                far_end(j - 2)

            return carry

        lax.fori_loop(1, batches + 2, steps, 0)
        x_copy.start()
        act_copy.start()

    def hidden_now(k):
        g_copy(k).wait_recv()
        gx_copy(k).start()
        g_now = g_own[rows_of(k), :]
        for h in range(2):
            part = mm(g_now, wot[h])
            hid_own[k, h] = part
            hid_send[k, h] = part.astype(jnp.bfloat16)
        for copy in hid_copies(k):
            copy.start()

    def back_now(k):
        for copy in hid_copies(k):
            copy.wait_recv()
        total = g_own[rows_of(k), :].astype(jnp.float32)
        for h in range(2):
            hidden = hid_own[k, h]
            for d in range(parts - 1):
                hidden = hidden + hid_recv[k, d, h].astype(jnp.float32)
            slice_d = (hidden * slope[h, rows_of(k), :]).astype(jnp.bfloat16)
            dpre[h, rows_of(k), :] = slice_d
            total = total + mm(slice_d, wit[h])
        back_ref[rows_of(k), :] = total.astype(jnp.bfloat16)

        @pl.when(section > 0)
        def _():
            g_copy(k).start()

        dx_start(k)

    near, early = pl.ds(0, rows // 2), pl.ds(0, rows - group)
    rest, late = pl.ds(rows // 2, rows // 2), pl.ds(rows - group, group)
    near_tiles = count // 2
    near_tile = width // near_tiles

    def own_tile(c):
        cols = span(c, near_tile)
        gin_acc[cols, :] = dot(x_own[near, cols], dpre[0, near, :], FIRST)
        gout_acc[:, cols] = dot(act[0, near, :], g_own[near, cols], FIRST)

    def chain(k, carry):
        @pl.when(k < count)
        def _():
            hidden_now(k)

        done = k - LAG

        @pl.when(done >= 0)
        def _():
            back_now(done)

        @pl.when(done >= count - near_tiles)
        def _():
            own_tile(done - (count - near_tiles))

        @pl.when(done == count - 2)
        def _():
            act_copy.wait_recv()
            for copy in pass_copies:
                copy.start()

        return carry

    @pl.when(section < pipes - 1)
    def _():
        act_copy.start()
        wo_copy.wait_recv()
        lax.fori_loop(0, count + LAG, chain, 0)

    @pl.when(first)
    def _():
        def all_own(c, carry):
            own_tile(c)
            return carry

        lax.fori_loop(0, near_tiles, all_own, 0)
        act_copy.wait_recv()
        for copy in pass_copies:
            copy.start()

    def move_on(i, carry):
        k = i * parts + me
        dx_copy(k).wait_recv()
        for copy in on_copies(k):
            copy.start()
        return carry

    lax.fori_loop(0, (count - tiles) // parts, move_on, 0)
    for copy in pass_copies:
        copy.wait_recv()

    def wait_gx(k, carry):
        gx_copy(k).wait_recv()
        return carry

    def wait_dx(k, carry):
        dx_copy(k).wait_recv()
        return carry

    @pl.when(section < pipes - 1)
    def _():
        lax.fori_loop(0, count - tiles, wait_gx, 0)

    def early_tile(c, carry):
        cols = span(c, tile)
        far_out = dot(act_other[early, :], g_other[early, cols], FIRST)
        gout_acc[:, cols] += dot(act[0, rest, :], g_own[rest, cols], FIRST) + far_out
        return carry

    lax.fori_loop(0, tiles, early_tile, 0)
    x_copy.wait_recv()

    def wait_on(k, carry):
        source = lax.rem(k, parts)

        @pl.when(source != me)
        def _():
            d = lax.rem(me - source + parts, parts) - 1
            r = rows_of(k)
            remote(dpre_other.at[r], dpre_other.at[r], on_ss.at[k, d], on_rs.at[k, d], partner).wait_recv()

        return carry

    lax.fori_loop(0, count - tiles, wait_on, 0)

    def early_in(c, carry):
        cols = span(c, tile)
        far_in = dot(x_other[early, cols], dpre_other[early, :], FIRST)
        gin_acc[cols, :] += dot(x_own[rest, cols], dpre[0, rest, :], FIRST) + far_in
        return carry

    lax.fori_loop(0, tiles, early_in, 0)

    for copy in [wi_copy, x_copy, act_copy] + pass_copies:
        copy.wait_send()

    @pl.when(section < pipes - 1)
    def _():
        wo_copy.wait_send()

    @pl.when(first)
    def _():
        for copy in top_copies():
            copy.wait_send()

        def drain_far(j, carry):
            for copy in far_copies(j) + over_copies(j):
                copy.wait_send()
            return carry

        lax.fori_loop(0, batches, drain_far, 0)

    for h in range(2):
        for copy in pre_copies(h) + full_copies(h):
            copy.wait_send()

    def sent_x(k, carry):
        gx_copy(k).wait_send()

        @pl.when(sends_dx(k))
        def _():
            dx_copy(k).wait_send()

        return carry

    def drain(k, carry):
        @pl.when((k < count - tiles) & (lax.rem(k, parts) == me))
        def _():
            for copy in on_copies(k):
                copy.wait_send()

        @pl.when(section < pipes - 1)
        def _():
            for copy in hid_copies(k):
                copy.wait_send()

        @pl.when(section > 0)
        def _():
            g_copy(k).wait_send()

        return carry

    lax.fori_loop(0, count, drain, 0)
    lax.fori_loop(0, count - tiles, sent_x, 0)

    @pl.when(section < pipes - 1)
    def _():
        lax.fori_loop(count - tiles, count, wait_gx, 0)

    lax.fori_loop(count - tiles, count, wait_dx, 0)

    def end_tile(c, carry):
        cols = span(c, tile)
        part_in = dot(x_other[late, cols], dpre_other[late, :], FIRST)
        part_out = dot(act_other[late, :], g_other[late, cols], FIRST)
        gin_ref[cols, :] = (gin_acc[cols, :] + part_in).astype(jnp.bfloat16)
        gout_ref[:, cols] = (gout_acc[:, cols] + part_out).astype(jnp.bfloat16)
        return carry

    lax.fori_loop(0, tiles, end_tile, 0)

    lax.fori_loop(count - tiles, count, sent_x, 0)


def flush(*refs):
    count = (len(refs) - 1) // 2
    sems = refs[-1]
    copies = []
    for i in range(count):
        src, dst = refs[i], refs[count + i]
        half = src.shape[0] // 2
        for j in range(2):
            r = pl.ds(j * half, half)
            copies.append(pltpu.make_async_copy(src.at[r], dst.at[r], sems.at[i, j]))
    for copy in copies:
        copy.start()
    for copy in copies:
        copy.wait()


def written(arrays):
    return pl.pallas_call(
        flush,
        out_shape=tuple(jax.ShapeDtypeStruct(a.shape, a.dtype) for a in arrays),
        in_specs=[pl.BlockSpec(memory_space=pltpu.VMEM)] * len(arrays),
        out_specs=tuple(pl.BlockSpec(memory_space=pl.ANY) for _ in arrays),
        scratch_shapes=[pltpu.SemaphoreType.DMA((len(arrays), 2))],
        compiler_params=pltpu.CompilerParams(vmem_limit_bytes=1024 * 1024),
    )(*arrays)


def pair_call(saved, w_in_now, w_out_now, top):
    pipes = lax.axis_size("pipe")
    parts = lax.axis_size("tensor")
    rows, width = saved.shape
    own = w_in_now.shape[1]
    count = rows // STEP
    share = rows // parts
    batches = rows // BATCH
    piece = BATCH // parts
    others = parts - 1
    bf, f32 = jnp.bfloat16, jnp.float32
    dma = pltpu.SemaphoreType.DMA
    vmem = pl.BlockSpec(memory_space=pltpu.VMEM)
    anywhere = pl.BlockSpec(memory_space=pl.ANY)
    return pl.pallas_call(
        functools.partial(paired, pipes, parts),
        out_shape=(
            jax.ShapeDtypeStruct((rows, width), bf),
            jax.ShapeDtypeStruct((width, own), bf),
            jax.ShapeDtypeStruct((own, width), bf),
        ),
        in_specs=[anywhere] * 4,
        out_specs=(vmem,) * 3,
        scratch_shapes=[
            pltpu.VMEM((rows, width), bf),
            pltpu.VMEM((rows, width), bf),
            pltpu.VMEM((width, own), bf),
            pltpu.VMEM((width, own), bf),
            pltpu.VMEM((own, width), bf),
            pltpu.VMEM((2, width, own), bf),
            pltpu.VMEM((2, own, width), bf),
            pltpu.VMEM((rows, width), bf),
            pltpu.VMEM((rows, width), bf),
            pltpu.VMEM((2, rows, own), f32),
            pltpu.VMEM((2, others, share, own), f32),
            pltpu.VMEM((2, rows, own), f32),
            pltpu.VMEM((2, rows, own), f32),
            pltpu.VMEM((2, rows, own), bf),
            pltpu.VMEM((rows, own), bf),
            pltpu.VMEM((2, rows, own), bf),
            pltpu.VMEM((rows, own), bf),
            pltpu.VMEM((count, 2, STEP, own), f32),
            pltpu.VMEM((count, 2, STEP, own), bf),
            pltpu.VMEM((count, others, 2, STEP, own), bf),
            pltpu.VMEM((width, own), f32),
            pltpu.VMEM((own, width), f32),
            pltpu.VMEM((rows, own), f32),
            pltpu.VMEM((rows, own), bf),
            pltpu.VMEM((others, rows, own), bf),
            pltpu.VMEM((batches, BATCH, own), f32),
            pltpu.VMEM((batches, others, piece, own), f32),
            pltpu.VMEM((batches, 2 * piece, own // 2), bf),
            pltpu.VMEM((batches, parts, 2 * piece, own // 2), bf),
            dma((others,)), dma((others,)),
            dma((batches, others)), dma((batches, others)),
            dma((batches, parts)), dma((batches, parts)),
            dma((others,)), dma((others,)), dma((count, others)), dma((count, others)),
            dma((4,)), dma((4,)), dma((4,)),
            dma((2, others)), dma((2, others)), dma((2, others)), dma((2, others)),
            dma((count, others)), dma((count, others)),
            dma((count,)), dma((count,)), dma((count,)), dma((count,)), dma((count,)), dma((count,)),
        ],
        compiler_params=pltpu.CompilerParams(
            collective_id=0, has_side_effects=True, vmem_limit_bytes=50 * 1024 * 1024
        ),
    )(saved, w_in_now, w_out_now, top)


def chain(
    pipes, parts, pair, chunks,
    x_ref, wi_ref, wo_ref, top_ref,
    back_ref, pin_ref, pout_ref,
    g_buf, pre_send, pre_recv, act_buf, hid_send, hid_recv, dpre_buf, slope_buf,
    pre_ss, pre_rs, act_ss, act_rs, hid_ss, hid_rs, dp_ss, dp_rs, g_ss, g_rs,
    *across,
):
    micro, rows, width = x_ref.shape
    own = wi_ref.shape[1]
    halves = 2 if pair else 1
    per = parts // halves
    quarter = own // per
    step_w = width // chunks
    section = lax.axis_index("pipe")
    me = lax.axis_index("tensor")
    first = section == pipes - 1
    below = jnp.maximum(section - 1, 0)
    above = jnp.minimum(section + 1, pipes - 1)
    peers = [lax.rem(me + d, parts) for d in range(1, parts)]

    barrier = pltpu.get_barrier_semaphore()
    for peer in peers:
        pl.semaphore_signal(barrier, inc=1, device_id={"tensor": peer}, device_id_type=MESH)
    if pair:
        partner = {"dp": 1 - lax.axis_index("dp")}
        pl.semaphore_signal(barrier, inc=1, device_id=partner, device_id_type=MESH)

    @pl.when(section > 0)
    def _():
        pl.semaphore_signal(barrier, inc=1, device_id={"pipe": below}, device_id_type=MESH)

    @pl.when(section < pipes - 1)
    def _():
        pl.semaphore_signal(barrier, inc=1, device_id={"pipe": above}, device_id_type=MESH)

    beside = jnp.minimum(section, 1) + jnp.minimum(pipes - 1 - section, 1)
    pl.semaphore_wait(barrier, parts - 1 + halves - 1 + beside)

    def remote(src, dst, send, recv, where):
        return pltpu.make_async_remote_copy(
            src_ref=src, dst_ref=dst, send_sem=send, recv_sem=recv,
            device_id=where, device_id_type=MESH,
        )

    wi_halves, wo_halves = [wi_ref], [wo_ref]
    if pair:
        wi_other, wo_other, x_other, g_other, dpre_other, act_other, one_ss, one_rs, gx_ss, gx_rs, dx_ss, dx_rs = across
        wi_halves.append(wi_other)
        wo_halves.append(wo_other)
        wi_copy = remote(wi_ref, wi_other, one_ss.at[0], one_rs.at[0], partner)
        wo_copy = remote(wo_ref, wo_other, one_ss.at[1], one_rs.at[1], partner)
        x_copy = remote(x_ref, x_other, one_ss.at[2], one_rs.at[2], partner)
        actx_copy = remote(act_buf.at[pl.ds(per, per)], act_other, one_ss.at[3], one_rs.at[3], partner)
        gx_copies = [remote(g_buf.at[m], g_other.at[m], gx_ss.at[m], gx_rs.at[m], partner) for m in range(micro)]
        dx_copies = [
            remote(dpre_buf.at[m, pl.ds(per, per)], dpre_other.at[m], dx_ss.at[m], dx_rs.at[m], partner)
            for m in range(micro)
        ]
        wi_copy.start()

    @pl.when(first)
    def _():
        g_buf[...] = top_ref[...]

    pre_copies = [
        remote(pre_send.at[peer], pre_recv.at[d], pre_ss.at[d], pre_rs.at[d], {"tensor": peer})
        for d, peer in enumerate(peers)
    ]
    hid_copies = [
        [
            remote(hid_send.at[m, peer], hid_recv.at[m, d], hid_ss.at[m, d], hid_rs.at[m, d], {"tensor": peer})
            for d, peer in enumerate(peers)
        ]
        for m in range(micro)
    ]
    dp_copies = [
        [
            remote(dpre_buf.at[m, me], dpre_buf.at[m, me], dp_ss.at[m, d], dp_rs.at[m, d], {"tensor": peer})
            for d, peer in enumerate(peers)
        ]
        for m in range(micro)
    ]
    act_copies = [
        remote(act_buf.at[me], act_buf.at[me], act_ss.at[d], act_rs.at[d], {"tensor": peer})
        for d, peer in enumerate(peers)
    ]
    g_copies = [
        [
            remote(
                back_ref.at[m, :, pl.ds(c * step_w, step_w)], g_buf.at[m, :, pl.ds(c * step_w, step_w)],
                g_ss.at[m, c], g_rs.at[m, c], {"pipe": below},
            )
            for c in range(chunks)
        ]
        for m in range(micro)
    ]

    flat_x = x_ref[...].reshape(micro * rows, width)
    for h in range(halves):
        if h == 1:
            wi_copy.wait_recv()
            wo_copy.start()
        pre = jnp.dot(flat_x, wi_halves[h][...], preferred_element_type=jnp.float32)
        for t in range(per):
            pre_send[h * per + t] = pre[:, t * quarter : (t + 1) * quarter]
    for copy in pre_copies:
        copy.start()

    def hidden_now(which):
        count = len(which)
        g_now = g_buf[which[0] : which[-1] + 1].reshape(count * rows, width)
        for h in range(halves):
            part = dot(g_now, wo_halves[h][...], LAST)
            for t in range(per):
                for i, m in enumerate(which):
                    hid_send[m, h * per + t] = part[i * rows : (i + 1) * rows, t * quarter : (t + 1) * quarter]
        for m in which:
            for copy in hid_copies[m]:
                copy.start()
        if pair:
            for m in which:
                gx_copies[m].start()

    def dpre_now(m):
        for copy in hid_copies[m]:
            copy.wait_recv()
        hidden = hid_send[m, me]
        for d in range(parts - 1):
            hidden = hidden + hid_recv[m, d]
        dpre_buf[m, me] = (hidden * slope_buf[m * rows : (m + 1) * rows, :]).astype(jnp.bfloat16)
        for copy in dp_copies[m]:
            copy.start()

    for copy in pre_copies:
        copy.wait_recv()
    mine = pre_send[me]
    for d in range(parts - 1):
        mine = mine + pre_recv[d]
    slope_buf[...] = silu_slope(mine)
    act_buf[me] = jax.nn.silu(mine).astype(jnp.bfloat16)
    for copy in act_copies:
        copy.start()

    if pair:
        wo_copy.wait_recv()
        x_copy.start()

    @pl.when(first)
    def _():
        hidden_now(list(range(micro)))
        for m in range(micro):
            dpre_now(m)

    for m in range(micro):
        @pl.when(section < pipes - 1)
        def _():
            for copy in g_copies[m]:
                copy.wait_recv()
            hidden_now([m])
            dpre_now(m)

        for copy in dp_copies[m]:
            copy.wait_recv()
        dpre_halves = [
            jnp.concatenate([dpre_buf[m, h * per + t] for t in range(per)], axis=1) for h in range(halves)
        ]
        for c in range(chunks):
            cols = pl.ds(c * step_w, step_w)
            total = g_buf[m, :, cols].astype(jnp.float32)
            for h in range(halves):
                total = total + dot(dpre_halves[h], wi_halves[h][cols, :], LAST)
            back_ref[m, :, cols] = total.astype(jnp.bfloat16)

            @pl.when(section > 0)
            def _():
                g_copies[m][c].start()

        if pair:
            dx_copies[m].start()
        if m == 0:
            for copy in act_copies:
                copy.wait_recv()
            if pair:
                actx_copy.start()

    sources = [(x_ref, g_buf, act_buf, dpre_buf)]
    if pair:
        x_copy.wait_recv()
        actx_copy.wait_recv()
        for m in range(micro):
            gx_copies[m].wait_recv()
            dx_copies[m].wait_recv()
        sources.append((x_other, g_other, act_other, dpre_other))
    ready = []
    for x_from, g_from, act_from, dpre_from in sources:
        act = jnp.concatenate([act_from[t] for t in range(per)], axis=1)
        dpre = jnp.concatenate(
            [dpre_from[:, t].reshape(micro * rows, quarter) for t in range(per)], axis=1
        )
        ready.append((x_from, g_from, act, dpre))

    for c in range(chunks):
        cols = pl.ds(c * step_w, step_w)
        grad_in, grad_out = 0.0, 0.0
        for x_from, g_from, act, dpre in ready:
            x_cols = x_from[:, :, cols].reshape(micro * rows, step_w)
            g_cols = g_from[:, :, cols].reshape(micro * rows, step_w)
            grad_in = grad_in + dot(x_cols, dpre, FIRST)
            grad_out = grad_out + dot(act, g_cols, FIRST)
        pin_ref[cols, :] = grad_in.astype(jnp.bfloat16)
        pout_ref[:, cols] = grad_out.astype(jnp.bfloat16)

    for copy in pre_copies + act_copies:
        copy.wait_send()
    if pair:
        for copy in [wi_copy, wo_copy, x_copy, actx_copy] + gx_copies + dx_copies:
            copy.wait_send()
    for m in range(micro):
        for copy in hid_copies[m] + dp_copies[m]:
            copy.wait_send()

        @pl.when(section > 0)
        def _():
            for copy in g_copies[m]:
                copy.wait_send()


def shards(acts, w_in, w_out, top_grad):
    pipes = lax.axis_size("pipe")
    parts = lax.axis_size("tensor")
    pair = lax.axis_size("dp") == 2 and parts % 2 == 0
    saved = acts[0]
    micro, rows, width = saved.shape
    if pair:
        out = written(pair_call(
            saved.reshape(micro * rows, width), w_in[0], w_out[0], top_grad.reshape(micro * rows, width)
        ))
        return out[0].reshape(1, micro, rows, width), out[1][None], out[2][None]
    if pair:
        w_in_now, w_out_now = w_in[0], w_out[0]
    else:
        w_in_now = lax.all_gather(w_in[0], "dp", axis=1, tiled=True)
        w_out_now = lax.all_gather(w_out[0], "dp", axis=0, tiled=True)
    own = w_in_now.shape[1]
    per = parts // 2 if pair else parts
    quarter = own // per
    chunks = 4
    others = parts - 1
    bf, f32 = jnp.bfloat16, jnp.float32
    dma = pltpu.SemaphoreType.DMA
    vmem = pl.BlockSpec(memory_space=pltpu.VMEM)
    across = []
    if pair:
        across = [
            pltpu.VMEM((width, own), bf),
            pltpu.VMEM((own, width), bf),
            pltpu.VMEM((micro, rows, width), bf),
            pltpu.VMEM((micro, rows, width), bf),
            pltpu.VMEM((micro, per, rows, quarter), bf),
            pltpu.VMEM((per, micro * rows, quarter), bf),
            dma((4,)), dma((4,)),
            dma((micro,)), dma((micro,)), dma((micro,)), dma((micro,)),
        ]
    back, grad_in, grad_out = pl.pallas_call(
        functools.partial(chain, pipes, parts, pair, chunks),
        out_shape=(
            jax.ShapeDtypeStruct((micro, rows, width), bf),
            jax.ShapeDtypeStruct((width, own), bf),
            jax.ShapeDtypeStruct((own, width), bf),
        ),
        in_specs=[vmem] * 4,
        out_specs=(vmem,) * 3,
        scratch_shapes=[
            pltpu.VMEM((micro, rows, width), bf),
            pltpu.VMEM((parts, micro * rows, quarter), f32),
            pltpu.VMEM((others, micro * rows, quarter), f32),
            pltpu.VMEM((parts, micro * rows, quarter), bf),
            pltpu.VMEM((micro, parts, rows, quarter), f32),
            pltpu.VMEM((micro, others, rows, quarter), f32),
            pltpu.VMEM((micro, parts, rows, quarter), bf),
            pltpu.VMEM((micro * rows, quarter), f32),
            dma((others,)), dma((others,)), dma((others,)), dma((others,)),
            dma((micro, others)), dma((micro, others)),
            dma((micro, others)), dma((micro, others)),
            dma((micro, chunks)), dma((micro, chunks)),
            *across,
        ],
        compiler_params=pltpu.CompilerParams(
            collective_id=0, has_side_effects=True, vmem_limit_bytes=48 * 1024 * 1024
        ),
    )(saved, w_in_now, w_out_now, top_grad)
    if not pair:
        grad_in = lax.psum_scatter(grad_in, "dp", scatter_dimension=1, tiled=True)
        grad_out = lax.psum_scatter(grad_out, "dp", scatter_dimension=0, tiled=True)
    return back[None], grad_in[None], grad_out[None]


def solution(mesh):
    placed = (
        P("pipe", None, "dp", "tensor"),
        P("pipe", "tensor", "dp"),
        P("pipe", "dp", "tensor"),
        P(None, "dp", "tensor"),
    )
    return jax.shard_map(
        shards,
        mesh=mesh,
        in_specs=placed,
        out_specs=(
            P("pipe", None, "dp", "tensor"),
            P("pipe", "tensor", "dp"),
            P("pipe", "dp", "tensor"),
        ),
        check_vma=False,
    )
```

```python
import functools

import jax
import jax.numpy as jnp
from jax import lax
from jax.experimental import pallas as pl
from jax.experimental.pallas import tpu as pltpu
from jax.sharding import PartitionSpec as P

MESH = pl.DeviceIdType.MESH
LAST = (((1,), (1,)), ((), ()))
FIRST = (((0,), (0,)), ((), ()))
STEP = 16
LAG = 2
AHEAD = 3
BATCH = 32


def silu_slope(value):
    sig = jax.nn.sigmoid(value)
    return sig * (1.0 + value * (1.0 - sig))


def dot(left, right, dims):
    return lax.dot_general(left, right, dims, preferred_element_type=jnp.float32)


def mm(left, right):
    return jnp.dot(left, right, preferred_element_type=jnp.float32)


def remote(src, dst, send, recv, where):
    return pltpu.make_async_remote_copy(
        src_ref=src, dst_ref=dst, send_sem=send, recv_sem=recv,
        device_id=where, device_id_type=MESH,
    )


def paired(
    pipes, parts,
    x_hbm, wi_hbm, wo_hbm, top_hbm,
    back_ref, gin_acc, gout_acc, x_other, g_other, act_other, dpre_other,
    x_own, wi_own, wi_other, wo_own, wot, wit, g_own,
    pre_part, pre_recv, pre_full, slope, act, dpre,
    hid_own, hid_send, hid_recv,
    top_part, top_send, top_recv, far_part, far_recv, far_send, far_hid,
    top_ss, top_rs, far_ss, far_rs, over_ss, over_rs,
    pass_ss, pass_rs, on_ss, on_rs,
    load_sem, bulk_ss, bulk_rs, pre_ss, pre_rs, full_ss, full_rs,
    hid_ss, hid_rs, g_ss, g_rs, gx_ss, gx_rs, dx_ss, dx_rs,
):
    rows, width = x_own.shape
    own = wi_own.shape[1]
    count = rows // STEP
    share = rows // parts
    section = lax.axis_index("pipe")
    me = lax.axis_index("tensor")
    first = section == pipes - 1
    last = section == 0
    below = jnp.maximum(section - 1, 0)
    above = jnp.minimum(section + 1, pipes - 1)
    peers = [lax.rem(me + d, parts) for d in range(1, parts)]
    other = 1 - lax.axis_index("dp")
    partner = {"dp": other}

    barrier = pltpu.get_barrier_semaphore()
    for peer in peers:
        pl.semaphore_signal(barrier, inc=1, device_id={"tensor": peer}, device_id_type=MESH)
    for peer in [me] + peers:
        pl.semaphore_signal(
            barrier, inc=1, device_id={"dp": other, "tensor": peer}, device_id_type=MESH
        )

    @pl.when(section > 0)
    def _():
        pl.semaphore_signal(barrier, inc=1, device_id={"pipe": below}, device_id_type=MESH)

    @pl.when(section < pipes - 1)
    def _():
        pl.semaphore_signal(barrier, inc=1, device_id={"pipe": above}, device_id_type=MESH)

    loads = [
        pltpu.make_async_copy(src, dst, load_sem.at[i])
        for i, (src, dst) in enumerate([(x_hbm, x_own), (wi_hbm, wi_own), (wo_hbm, wo_own), (top_hbm, g_own)])
    ]
    for copy in loads[:3]:
        copy.start()

    @pl.when(first)
    def _():
        loads[3].start()

    beside = jnp.minimum(section, 1) + jnp.minimum(pipes - 1 - section, 1)
    pl.semaphore_wait(barrier, 2 * parts - 1 + beside)

    wi_copy = remote(wi_hbm, wi_other, bulk_ss.at[0], bulk_rs.at[0], partner)
    wo_copy = remote(wot.at[0], wot.at[1], bulk_ss.at[1], bulk_rs.at[1], partner)
    x_copy = remote(x_hbm, x_other, bulk_ss.at[2], bulk_rs.at[2], partner)
    my_share = pl.ds(pl.multiple_of(me * share, share), share)
    act_copy = remote(act.at[1, my_share], act_other.at[my_share], bulk_ss.at[3], bulk_rs.at[3], partner)
    pass_copies = [
        remote(act_other.at[my_share], act_other.at[my_share], pass_ss.at[d], pass_rs.at[d], {"tensor": peer})
        for d, peer in enumerate(peers)
    ]
    wi_copy.start()

    loads[2].wait()

    def turn_out(b, carry):
        cols = pl.ds(pl.multiple_of(b * 256, 256), 256)
        wot[0, cols, :] = wo_own[:, cols].T
        return carry

    lax.fori_loop(0, width // 256, turn_out, 0)

    @pl.when(section < pipes - 1)
    def _():
        wo_copy.start()
        x_copy.start()

    tile = 512
    tiles = width // tile
    group = tiles * STEP

    def rows_of(k):
        return pl.ds(pl.multiple_of(k * STEP, STEP), STEP)

    def g_copy(k):
        return remote(back_ref.at[rows_of(k)], g_own.at[rows_of(k)], g_ss.at[k], g_rs.at[k], {"pipe": below})

    def gx_copy(k):
        return remote(g_own.at[rows_of(k)], g_other.at[rows_of(k)], gx_ss.at[k], gx_rs.at[k], partner)

    def dx_copy(k):
        return remote(dpre.at[1, rows_of(k)], dpre_other.at[rows_of(k)], dx_ss.at[k], dx_rs.at[k], partner)

    def sends_dx(k):
        return (k >= count - tiles) | (lax.rem(k, parts) == me)

    def dx_start(k):
        @pl.when(sends_dx(k))
        def _():
            dx_copy(k).start()

    def on_copies(k):
        r = rows_of(k)
        return [
            remote(dpre_other.at[r], dpre_other.at[r], on_ss.at[k, d], on_rs.at[k, d], {"tensor": peer})
            for d, peer in enumerate(peers)
        ]

    def hid_copies(k):
        return [
            remote(hid_send.at[k], hid_recv.at[k, d], hid_ss.at[k, d], hid_rs.at[k, d], {"tensor": peer})
            for d, peer in enumerate(peers)
        ]

    per_batch = BATCH // STEP
    batch = BATCH
    piece = batch // parts
    batches = rows // batch

    def span(j, size):
        return pl.ds(pl.multiple_of(j * size, size), size)

    def top_copies():
        return [
            remote(top_send, top_recv.at[d], top_ss.at[d], top_rs.at[d], {"tensor": peer})
            for d, peer in enumerate(peers)
        ]

    def far_copies(j):
        return [
            remote(
                far_part.at[j, pl.ds(peer * piece, piece)], far_recv.at[j, d],
                far_ss.at[j, d], far_rs.at[j, d], {"tensor": peer},
            )
            for d, peer in enumerate(peers)
        ]

    def over_copies(j):
        return [
            remote(
                far_send.at[j], far_hid.at[j, d],
                over_ss.at[j, d], over_rs.at[j, d], {"dp": other, "tensor": peer},
            )
            for d, peer in enumerate([me] + peers)
        ]

    def send_top(j):
        for i in range(per_batch):
            gx_copy(per_batch * j + i).start()

    def far_start(j):
        for i in range(per_batch):
            gx_copy(per_batch * j + i).wait_recv()
        far_part[j] = mm(g_other[span(j, batch), :], wot[0])
        for copy in far_copies(j):
            copy.start()

    def far_sum(j):
        for copy in far_copies(j):
            copy.wait_recv()
        total = far_part[j, pl.ds(pl.multiple_of(me * piece, piece), piece), :]
        for d in range(parts - 1):
            total = total + far_recv[j, d]
        half = own // 2
        far_send[j] = jnp.concatenate([total[:, :half], total[:, half:]], axis=0).astype(jnp.bfloat16)
        for copy in over_copies(j):
            copy.start()

    def far_end(j):
        for copy in over_copies(j):
            copy.wait_recv()
        r = span(j, batch)
        near = top_part[r, :]
        for d in range(parts - 1):
            near = near + top_recv[d, r, :].astype(jnp.float32)
        total = g_own[r, :].astype(jnp.float32)
        slice_d = (near * slope[0, r, :]).astype(jnp.bfloat16)
        dpre[0, r, :] = slice_d
        total = total + mm(slice_d, wit[0])
        parts_now = []
        for t in range(parts):
            d = lax.rem(me - t + parts, parts)
            got = far_hid[j, d].astype(jnp.float32)
            parts_now.append(jnp.concatenate([got[:piece], got[piece:]], axis=1))
        slice_d = (jnp.concatenate(parts_now, axis=0) * slope[1, r, :]).astype(jnp.bfloat16)
        dpre[1, r, :] = slice_d
        total = total + mm(slice_d, wit[1])
        back_ref[r, :] = total.astype(jnp.bfloat16)
        for i in range(per_batch):
            g_copy(per_batch * j + i).start()
            dx_start(per_batch * j + i)

    def pre_copies(h):
        return [
            remote(
                pre_part.at[h, pl.ds(peer * share, share)], pre_recv.at[h, d],
                pre_ss.at[h, d], pre_rs.at[h, d], {"tensor": peer},
            )
            for d, peer in enumerate(peers)
        ]

    def full_copies(h):
        mine = pl.ds(me * share, share)
        return [
            remote(
                pre_full.at[h, mine], pre_full.at[h, mine],
                full_ss.at[h, d], full_rs.at[h, d], {"tensor": peer},
            )
            for d, peer in enumerate(peers)
        ]

    def turn_in(h, src):
        def body(b, carry):
            cols = pl.ds(pl.multiple_of(b * 256, 256), 256)
            wit[h, :, cols] = src[cols, :].T
            return carry

        lax.fori_loop(0, width // 256, body, 0)

    def pre_start(h, src):
        pre_part[h] = mm(x_own[...], src[...])
        for copy in pre_copies(h):
            copy.start()

    def pre_sum(h):
        for copy in pre_copies(h):
            copy.wait_recv()
        mine = pl.ds(pl.multiple_of(me * share, share), share)
        total = pre_part[h, mine, :]
        for d in range(parts - 1):
            total = total + pre_recv[h, d]
        pre_full[h, mine, :] = total
        for copy in full_copies(h):
            copy.start()

    def pre_end(h):
        for copy in full_copies(h):
            copy.wait_recv()
        value = pre_full[h]
        slope[h] = silu_slope(value)
        act[h] = jax.nn.silu(value).astype(jnp.bfloat16)

    @pl.when(first)
    def _():
        loads[3].wait()

        for j in range(AHEAD):
            send_top(j)
        near = mm(g_own[...], wot[0])
        top_part[...] = near
        top_send[...] = near.astype(jnp.bfloat16)
        for copy in top_copies():
            copy.start()

    loads[0].wait()
    loads[1].wait()
    pre_start(0, wi_own)
    turn_in(0, wi_own)
    pre_sum(0)
    pre_end(0)
    wi_copy.wait_recv()
    pre_start(1, wi_other)
    turn_in(1, wi_other)
    pre_sum(1)

    @pl.when(first)
    def _():
        far_start(0)
        send_top(AHEAD)
        for copy in top_copies():
            copy.wait_recv()

    pre_end(1)

    @pl.when(first)
    def _():
        def steps(j, carry):
            @pl.when(j < batches)
            def _():
                far_start(j)

                @pl.when(j + AHEAD < batches)
                def _():
                    send_top(j + AHEAD)

            @pl.when(j <= batches)
            def _():
                far_sum(j - 1)

            @pl.when(j >= 2)
            def _():
                far_end(j - 2)

            return carry

        lax.fori_loop(1, batches + 2, steps, 0)
        x_copy.start()
        act_copy.start()

    def hidden_now(k):
        g_copy(k).wait_recv()
        gx_copy(k).start()
        g_now = g_own[rows_of(k), :]
        for h in range(2):
            part = mm(g_now, wot[h])
            hid_own[k, h] = part
            hid_send[k, h] = part.astype(jnp.bfloat16)
        for copy in hid_copies(k):
            copy.start()

    def back_now(k):
        for copy in hid_copies(k):
            copy.wait_recv()
        total = g_own[rows_of(k), :].astype(jnp.float32)
        for h in range(2):
            hidden = hid_own[k, h]
            for d in range(parts - 1):
                hidden = hidden + hid_recv[k, d, h].astype(jnp.float32)
            slice_d = (hidden * slope[h, rows_of(k), :]).astype(jnp.bfloat16)
            dpre[h, rows_of(k), :] = slice_d
            total = total + mm(slice_d, wit[h])
        back_ref[rows_of(k), :] = total.astype(jnp.bfloat16)

        @pl.when(section > 0)
        def _():
            g_copy(k).start()

        dx_start(k)

    near, early = pl.ds(0, rows // 2), pl.ds(0, rows - group)
    rest, late = pl.ds(rows // 2, rows // 2), pl.ds(rows - group, group)
    near_tiles = count // 2
    near_tile = width // near_tiles

    def own_tile(c):
        cols = span(c, near_tile)
        gin_acc[cols, :] = dot(x_own[near, cols], dpre[0, near, :], FIRST)
        gout_acc[:, cols] = dot(act[0, near, :], g_own[near, cols], FIRST)

    def chain(k, carry):
        @pl.when(k < count)
        def _():
            hidden_now(k)

        done = k - LAG

        @pl.when(done >= 0)
        def _():
            back_now(done)

        @pl.when(done >= count - near_tiles)
        def _():
            own_tile(done - (count - near_tiles))

        @pl.when(done == count - 2)
        def _():
            act_copy.wait_recv()
            for copy in pass_copies:
                copy.start()

        return carry

    @pl.when(section < pipes - 1)
    def _():
        act_copy.start()
        wo_copy.wait_recv()
        lax.fori_loop(0, count + LAG, chain, 0)

    @pl.when(first)
    def _():
        def all_own(c, carry):
            own_tile(c)
            return carry

        lax.fori_loop(0, near_tiles, all_own, 0)
        act_copy.wait_recv()
        for copy in pass_copies:
            copy.start()

    def move_on(i, carry):
        k = i * parts + me
        dx_copy(k).wait_recv()
        for copy in on_copies(k):
            copy.start()
        return carry

    lax.fori_loop(0, (count - tiles) // parts, move_on, 0)
    for copy in pass_copies:
        copy.wait_recv()

    def wait_gx(k, carry):
        gx_copy(k).wait_recv()
        return carry

    def wait_dx(k, carry):
        dx_copy(k).wait_recv()
        return carry

    @pl.when(section < pipes - 1)
    def _():
        lax.fori_loop(0, count - tiles, wait_gx, 0)

    def early_tile(c, carry):
        cols = span(c, tile)
        far_out = dot(act_other[early, :], g_other[early, cols], FIRST)
        gout_acc[:, cols] += dot(act[0, rest, :], g_own[rest, cols], FIRST) + far_out
        return carry

    lax.fori_loop(0, tiles, early_tile, 0)
    x_copy.wait_recv()

    def wait_on(k, carry):
        source = lax.rem(k, parts)

        @pl.when(source != me)
        def _():
            d = lax.rem(me - source + parts, parts) - 1
            r = rows_of(k)
            remote(dpre_other.at[r], dpre_other.at[r], on_ss.at[k, d], on_rs.at[k, d], partner).wait_recv()

        return carry

    lax.fori_loop(0, count - tiles, wait_on, 0)

    def early_in(c, carry):
        cols = span(c, tile)
        far_in = dot(x_other[early, cols], dpre_other[early, :], FIRST)
        gin_acc[cols, :] += dot(x_own[rest, cols], dpre[0, rest, :], FIRST) + far_in
        return carry

    lax.fori_loop(0, tiles, early_in, 0)

    for copy in [wi_copy, x_copy, act_copy] + pass_copies:
        copy.wait_send()

    @pl.when(section < pipes - 1)
    def _():
        wo_copy.wait_send()

    @pl.when(first)
    def _():
        for copy in top_copies():
            copy.wait_send()

        def drain_far(j, carry):
            for copy in far_copies(j) + over_copies(j):
                copy.wait_send()
            return carry

        lax.fori_loop(0, batches, drain_far, 0)

    for h in range(2):
        for copy in pre_copies(h) + full_copies(h):
            copy.wait_send()

    def sent_x(k, carry):
        gx_copy(k).wait_send()

        @pl.when(sends_dx(k))
        def _():
            dx_copy(k).wait_send()

        return carry

    def drain(k, carry):
        @pl.when((k < count - tiles) & (lax.rem(k, parts) == me))
        def _():
            for copy in on_copies(k):
                copy.wait_send()

        @pl.when(section < pipes - 1)
        def _():
            for copy in hid_copies(k):
                copy.wait_send()

        @pl.when(section > 0)
        def _():
            g_copy(k).wait_send()

        return carry

    lax.fori_loop(0, count, drain, 0)
    lax.fori_loop(0, count - tiles, sent_x, 0)

    @pl.when(section < pipes - 1)
    def _():
        lax.fori_loop(count - tiles, count, wait_gx, 0)

    lax.fori_loop(count - tiles, count, wait_dx, 0)

    lax.fori_loop(count - tiles, count, sent_x, 0)


def finish(
    late, tile,
    back_ref, gin_acc, gout_acc, x_other, g_other, act_other, dpre_other,
    back_out, gin_out, gout_out, gin_part, gout_part, sems,
):
    rows, width = x_other.shape
    tiles = width // tile
    r = pl.ds(rows - late, late)
    half = rows // 2
    copies = []
    for j in range(2):
        part = pl.ds(j * half, half)
        copies.append(pltpu.make_async_copy(back_ref.at[part], back_out.at[part], sems.at[0, j]))
        copies[-1].start()
    for c in range(tiles):
        cols = pl.ds(c * tile, tile)
        gin_part[cols, :] = (gin_acc[cols, :] + dot(x_other[r, cols], dpre_other[r, :], FIRST)).astype(jnp.bfloat16)
        copies.append(pltpu.make_async_copy(gin_part.at[cols], gin_out.at[cols], sems.at[1, c]))
        copies[-1].start()
        gout_part[:, cols] = (gout_acc[:, cols] + dot(act_other[r, :], g_other[r, cols], FIRST)).astype(jnp.bfloat16)
        copies.append(pltpu.make_async_copy(gout_part.at[:, cols], gout_out.at[:, cols], sems.at[2, c]))
        copies[-1].start()
    for copy in copies:
        copy.wait()


def written(arrays):
    back, gin, gout = arrays[:3]
    tile = 512
    tiles = back.shape[1] // tile
    bf = jnp.bfloat16
    shapes = (back.shape, gin.shape, gout.shape)
    return pl.pallas_call(
        functools.partial(finish, tiles * STEP, tile),
        out_shape=tuple(jax.ShapeDtypeStruct(shape, bf) for shape in shapes),
        in_specs=[pl.BlockSpec(memory_space=pltpu.VMEM)] * len(arrays),
        out_specs=tuple(pl.BlockSpec(memory_space=pl.ANY) for _ in shapes),
        scratch_shapes=[
            pltpu.VMEM(gin.shape, bf), pltpu.VMEM(gout.shape, bf),
            pltpu.SemaphoreType.DMA((3, tiles)),
        ],
        compiler_params=pltpu.CompilerParams(vmem_limit_bytes=8 * 1024 * 1024),
    )(*arrays)


def pair_call(saved, w_in_now, w_out_now, top):
    pipes = lax.axis_size("pipe")
    parts = lax.axis_size("tensor")
    rows, width = saved.shape
    own = w_in_now.shape[1]
    count = rows // STEP
    share = rows // parts
    batches = rows // BATCH
    piece = BATCH // parts
    others = parts - 1
    bf, f32 = jnp.bfloat16, jnp.float32
    dma = pltpu.SemaphoreType.DMA
    vmem = pl.BlockSpec(memory_space=pltpu.VMEM)
    anywhere = pl.BlockSpec(memory_space=pl.ANY)
    return pl.pallas_call(
        functools.partial(paired, pipes, parts),
        out_shape=(
            jax.ShapeDtypeStruct((rows, width), bf),
            jax.ShapeDtypeStruct((width, own), f32),
            jax.ShapeDtypeStruct((own, width), f32),
            jax.ShapeDtypeStruct((rows, width), bf),
            jax.ShapeDtypeStruct((rows, width), bf),
            jax.ShapeDtypeStruct((rows, own), bf),
            jax.ShapeDtypeStruct((rows, own), bf),
        ),
        in_specs=[anywhere] * 4,
        out_specs=(vmem,) * 7,
        scratch_shapes=[
            pltpu.VMEM((rows, width), bf),
            pltpu.VMEM((width, own), bf),
            pltpu.VMEM((width, own), bf),
            pltpu.VMEM((own, width), bf),
            pltpu.VMEM((2, width, own), bf),
            pltpu.VMEM((2, own, width), bf),
            pltpu.VMEM((rows, width), bf),
            pltpu.VMEM((2, rows, own), f32),
            pltpu.VMEM((2, others, share, own), f32),
            pltpu.VMEM((2, rows, own), f32),
            pltpu.VMEM((2, rows, own), f32),
            pltpu.VMEM((2, rows, own), bf),
            pltpu.VMEM((2, rows, own), bf),
            pltpu.VMEM((count, 2, STEP, own), f32),
            pltpu.VMEM((count, 2, STEP, own), bf),
            pltpu.VMEM((count, others, 2, STEP, own), bf),
            pltpu.VMEM((rows, own), f32),
            pltpu.VMEM((rows, own), bf),
            pltpu.VMEM((others, rows, own), bf),
            pltpu.VMEM((batches, BATCH, own), f32),
            pltpu.VMEM((batches, others, piece, own), f32),
            pltpu.VMEM((batches, 2 * piece, own // 2), bf),
            pltpu.VMEM((batches, parts, 2 * piece, own // 2), bf),
            dma((others,)), dma((others,)),
            dma((batches, others)), dma((batches, others)),
            dma((batches, parts)), dma((batches, parts)),
            dma((others,)), dma((others,)), dma((count, others)), dma((count, others)),
            dma((4,)), dma((4,)), dma((4,)),
            dma((2, others)), dma((2, others)), dma((2, others)), dma((2, others)),
            dma((count, others)), dma((count, others)),
            dma((count,)), dma((count,)), dma((count,)), dma((count,)), dma((count,)), dma((count,)),
        ],
        compiler_params=pltpu.CompilerParams(
            collective_id=0, has_side_effects=True, vmem_limit_bytes=42 * 1024 * 1024
        ),
    )(*[pltpu.with_memory_space_constraint(a, pltpu.HBM) for a in (saved, w_in_now, w_out_now, top)])


def chain(
    pipes, parts, pair, chunks,
    x_ref, wi_ref, wo_ref, top_ref,
    back_ref, pin_ref, pout_ref,
    g_buf, pre_send, pre_recv, act_buf, hid_send, hid_recv, dpre_buf, slope_buf,
    pre_ss, pre_rs, act_ss, act_rs, hid_ss, hid_rs, dp_ss, dp_rs, g_ss, g_rs,
    *across,
):
    micro, rows, width = x_ref.shape
    own = wi_ref.shape[1]
    halves = 2 if pair else 1
    per = parts // halves
    quarter = own // per
    step_w = width // chunks
    section = lax.axis_index("pipe")
    me = lax.axis_index("tensor")
    first = section == pipes - 1
    below = jnp.maximum(section - 1, 0)
    above = jnp.minimum(section + 1, pipes - 1)
    peers = [lax.rem(me + d, parts) for d in range(1, parts)]

    barrier = pltpu.get_barrier_semaphore()
    for peer in peers:
        pl.semaphore_signal(barrier, inc=1, device_id={"tensor": peer}, device_id_type=MESH)
    if pair:
        partner = {"dp": 1 - lax.axis_index("dp")}
        pl.semaphore_signal(barrier, inc=1, device_id=partner, device_id_type=MESH)

    @pl.when(section > 0)
    def _():
        pl.semaphore_signal(barrier, inc=1, device_id={"pipe": below}, device_id_type=MESH)

    @pl.when(section < pipes - 1)
    def _():
        pl.semaphore_signal(barrier, inc=1, device_id={"pipe": above}, device_id_type=MESH)

    beside = jnp.minimum(section, 1) + jnp.minimum(pipes - 1 - section, 1)
    pl.semaphore_wait(barrier, parts - 1 + halves - 1 + beside)

    def remote(src, dst, send, recv, where):
        return pltpu.make_async_remote_copy(
            src_ref=src, dst_ref=dst, send_sem=send, recv_sem=recv,
            device_id=where, device_id_type=MESH,
        )

    wi_halves, wo_halves = [wi_ref], [wo_ref]
    if pair:
        wi_other, wo_other, x_other, g_other, dpre_other, act_other, one_ss, one_rs, gx_ss, gx_rs, dx_ss, dx_rs = across
        wi_halves.append(wi_other)
        wo_halves.append(wo_other)
        wi_copy = remote(wi_ref, wi_other, one_ss.at[0], one_rs.at[0], partner)
        wo_copy = remote(wo_ref, wo_other, one_ss.at[1], one_rs.at[1], partner)
        x_copy = remote(x_ref, x_other, one_ss.at[2], one_rs.at[2], partner)
        actx_copy = remote(act_buf.at[pl.ds(per, per)], act_other, one_ss.at[3], one_rs.at[3], partner)
        gx_copies = [remote(g_buf.at[m], g_other.at[m], gx_ss.at[m], gx_rs.at[m], partner) for m in range(micro)]
        dx_copies = [
            remote(dpre_buf.at[m, pl.ds(per, per)], dpre_other.at[m], dx_ss.at[m], dx_rs.at[m], partner)
            for m in range(micro)
        ]
        wi_copy.start()

    @pl.when(first)
    def _():
        g_buf[...] = top_ref[...]

    pre_copies = [
        remote(pre_send.at[peer], pre_recv.at[d], pre_ss.at[d], pre_rs.at[d], {"tensor": peer})
        for d, peer in enumerate(peers)
    ]
    hid_copies = [
        [
            remote(hid_send.at[m, peer], hid_recv.at[m, d], hid_ss.at[m, d], hid_rs.at[m, d], {"tensor": peer})
            for d, peer in enumerate(peers)
        ]
        for m in range(micro)
    ]
    dp_copies = [
        [
            remote(dpre_buf.at[m, me], dpre_buf.at[m, me], dp_ss.at[m, d], dp_rs.at[m, d], {"tensor": peer})
            for d, peer in enumerate(peers)
        ]
        for m in range(micro)
    ]
    act_copies = [
        remote(act_buf.at[me], act_buf.at[me], act_ss.at[d], act_rs.at[d], {"tensor": peer})
        for d, peer in enumerate(peers)
    ]
    g_copies = [
        [
            remote(
                back_ref.at[m, :, pl.ds(c * step_w, step_w)], g_buf.at[m, :, pl.ds(c * step_w, step_w)],
                g_ss.at[m, c], g_rs.at[m, c], {"pipe": below},
            )
            for c in range(chunks)
        ]
        for m in range(micro)
    ]

    flat_x = x_ref[...].reshape(micro * rows, width)
    for h in range(halves):
        if h == 1:
            wi_copy.wait_recv()
            wo_copy.start()
        pre = jnp.dot(flat_x, wi_halves[h][...], preferred_element_type=jnp.float32)
        for t in range(per):
            pre_send[h * per + t] = pre[:, t * quarter : (t + 1) * quarter]
    for copy in pre_copies:
        copy.start()

    def hidden_now(which):
        count = len(which)
        g_now = g_buf[which[0] : which[-1] + 1].reshape(count * rows, width)
        for h in range(halves):
            part = dot(g_now, wo_halves[h][...], LAST)
            for t in range(per):
                for i, m in enumerate(which):
                    hid_send[m, h * per + t] = part[i * rows : (i + 1) * rows, t * quarter : (t + 1) * quarter]
        for m in which:
            for copy in hid_copies[m]:
                copy.start()
        if pair:
            for m in which:
                gx_copies[m].start()

    def dpre_now(m):
        for copy in hid_copies[m]:
            copy.wait_recv()
        hidden = hid_send[m, me]
        for d in range(parts - 1):
            hidden = hidden + hid_recv[m, d]
        dpre_buf[m, me] = (hidden * slope_buf[m * rows : (m + 1) * rows, :]).astype(jnp.bfloat16)
        for copy in dp_copies[m]:
            copy.start()

    for copy in pre_copies:
        copy.wait_recv()
    mine = pre_send[me]
    for d in range(parts - 1):
        mine = mine + pre_recv[d]
    slope_buf[...] = silu_slope(mine)
    act_buf[me] = jax.nn.silu(mine).astype(jnp.bfloat16)
    for copy in act_copies:
        copy.start()

    if pair:
        wo_copy.wait_recv()
        x_copy.start()

    @pl.when(first)
    def _():
        hidden_now(list(range(micro)))
        for m in range(micro):
            dpre_now(m)

    for m in range(micro):
        @pl.when(section < pipes - 1)
        def _():
            for copy in g_copies[m]:
                copy.wait_recv()
            hidden_now([m])
            dpre_now(m)

        for copy in dp_copies[m]:
            copy.wait_recv()
        dpre_halves = [
            jnp.concatenate([dpre_buf[m, h * per + t] for t in range(per)], axis=1) for h in range(halves)
        ]
        for c in range(chunks):
            cols = pl.ds(c * step_w, step_w)
            total = g_buf[m, :, cols].astype(jnp.float32)
            for h in range(halves):
                total = total + dot(dpre_halves[h], wi_halves[h][cols, :], LAST)
            back_ref[m, :, cols] = total.astype(jnp.bfloat16)

            @pl.when(section > 0)
            def _():
                g_copies[m][c].start()

        if pair:
            dx_copies[m].start()
        if m == 0:
            for copy in act_copies:
                copy.wait_recv()
            if pair:
                actx_copy.start()

    sources = [(x_ref, g_buf, act_buf, dpre_buf)]
    if pair:
        x_copy.wait_recv()
        actx_copy.wait_recv()
        for m in range(micro):
            gx_copies[m].wait_recv()
            dx_copies[m].wait_recv()
        sources.append((x_other, g_other, act_other, dpre_other))
    ready = []
    for x_from, g_from, act_from, dpre_from in sources:
        act = jnp.concatenate([act_from[t] for t in range(per)], axis=1)
        dpre = jnp.concatenate(
            [dpre_from[:, t].reshape(micro * rows, quarter) for t in range(per)], axis=1
        )
        ready.append((x_from, g_from, act, dpre))

    for c in range(chunks):
        cols = pl.ds(c * step_w, step_w)
        grad_in, grad_out = 0.0, 0.0
        for x_from, g_from, act, dpre in ready:
            x_cols = x_from[:, :, cols].reshape(micro * rows, step_w)
            g_cols = g_from[:, :, cols].reshape(micro * rows, step_w)
            grad_in = grad_in + dot(x_cols, dpre, FIRST)
            grad_out = grad_out + dot(act, g_cols, FIRST)
        pin_ref[cols, :] = grad_in.astype(jnp.bfloat16)
        pout_ref[:, cols] = grad_out.astype(jnp.bfloat16)

    for copy in pre_copies + act_copies:
        copy.wait_send()
    if pair:
        for copy in [wi_copy, wo_copy, x_copy, actx_copy] + gx_copies + dx_copies:
            copy.wait_send()
    for m in range(micro):
        for copy in hid_copies[m] + dp_copies[m]:
            copy.wait_send()

        @pl.when(section > 0)
        def _():
            for copy in g_copies[m]:
                copy.wait_send()


def shards(acts, w_in, w_out, top_grad):
    pipes = lax.axis_size("pipe")
    parts = lax.axis_size("tensor")
    pair = lax.axis_size("dp") == 2 and parts % 2 == 0
    saved = acts[0]
    micro, rows, width = saved.shape
    if pair:
        out = written(pair_call(
            saved.reshape(micro * rows, width), w_in[0], w_out[0], top_grad.reshape(micro * rows, width)
        ))
        return out[0].reshape(1, micro, rows, width), out[1][None], out[2][None]
    if pair:
        w_in_now, w_out_now = w_in[0], w_out[0]
    else:
        w_in_now = lax.all_gather(w_in[0], "dp", axis=1, tiled=True)
        w_out_now = lax.all_gather(w_out[0], "dp", axis=0, tiled=True)
    own = w_in_now.shape[1]
    per = parts // 2 if pair else parts
    quarter = own // per
    chunks = 4
    others = parts - 1
    bf, f32 = jnp.bfloat16, jnp.float32
    dma = pltpu.SemaphoreType.DMA
    vmem = pl.BlockSpec(memory_space=pltpu.VMEM)
    across = []
    if pair:
        across = [
            pltpu.VMEM((width, own), bf),
            pltpu.VMEM((own, width), bf),
            pltpu.VMEM((micro, rows, width), bf),
            pltpu.VMEM((micro, rows, width), bf),
            pltpu.VMEM((micro, per, rows, quarter), bf),
            pltpu.VMEM((per, micro * rows, quarter), bf),
            dma((4,)), dma((4,)),
            dma((micro,)), dma((micro,)), dma((micro,)), dma((micro,)),
        ]
    back, grad_in, grad_out = pl.pallas_call(
        functools.partial(chain, pipes, parts, pair, chunks),
        out_shape=(
            jax.ShapeDtypeStruct((micro, rows, width), bf),
            jax.ShapeDtypeStruct((width, own), bf),
            jax.ShapeDtypeStruct((own, width), bf),
        ),
        in_specs=[vmem] * 4,
        out_specs=(vmem,) * 3,
        scratch_shapes=[
            pltpu.VMEM((micro, rows, width), bf),
            pltpu.VMEM((parts, micro * rows, quarter), f32),
            pltpu.VMEM((others, micro * rows, quarter), f32),
            pltpu.VMEM((parts, micro * rows, quarter), bf),
            pltpu.VMEM((micro, parts, rows, quarter), f32),
            pltpu.VMEM((micro, others, rows, quarter), f32),
            pltpu.VMEM((micro, parts, rows, quarter), bf),
            pltpu.VMEM((micro * rows, quarter), f32),
            dma((others,)), dma((others,)), dma((others,)), dma((others,)),
            dma((micro, others)), dma((micro, others)),
            dma((micro, others)), dma((micro, others)),
            dma((micro, chunks)), dma((micro, chunks)),
            *across,
        ],
        compiler_params=pltpu.CompilerParams(
            collective_id=0, has_side_effects=True, vmem_limit_bytes=48 * 1024 * 1024
        ),
    )(saved, w_in_now, w_out_now, top_grad)
    if not pair:
        grad_in = lax.psum_scatter(grad_in, "dp", scatter_dimension=1, tiled=True)
        grad_out = lax.psum_scatter(grad_out, "dp", scatter_dimension=0, tiled=True)
    return back[None], grad_in[None], grad_out[None]


def solution(mesh):
    placed = (
        P("pipe", None, "dp", "tensor"),
        P("pipe", "tensor", "dp"),
        P("pipe", "dp", "tensor"),
        P(None, "dp", "tensor"),
    )
    return jax.shard_map(
        shards,
        mesh=mesh,
        in_specs=placed,
        out_specs=(
            P("pipe", None, "dp", "tensor"),
            P("pipe", "tensor", "dp"),
            P("pipe", "dp", "tensor"),
        ),
        check_vma=False,
    )
```

```python
import functools

import jax
import jax.numpy as jnp
from jax import lax
from jax.experimental import pallas as pl
from jax.experimental.pallas import tpu as pltpu
from jax.sharding import PartitionSpec as P

MESH = pl.DeviceIdType.MESH
LAST = (((1,), (1,)), ((), ()))
FIRST = (((0,), (0,)), ((), ()))
STEP = 16
LAG = 2
AHEAD = 3
BATCH = 32


def silu_slope(value):
    sig = jax.nn.sigmoid(value)
    return sig * (1.0 + value * (1.0 - sig))


def dot(left, right, dims):
    return lax.dot_general(left, right, dims, preferred_element_type=jnp.float32)


def mm(left, right):
    return jnp.dot(left, right, preferred_element_type=jnp.float32)


def remote(src, dst, send, recv, where):
    return pltpu.make_async_remote_copy(
        src_ref=src, dst_ref=dst, send_sem=send, recv_sem=recv,
        device_id=where, device_id_type=MESH,
    )


def paired(
    pipes, parts,
    x_hbm, wi_hbm, wo_hbm, top_hbm,
    back_ref, gin_acc, gout_acc, x_other, g_other, act_other, dpre_other,
    x_own, wi_own, wi_other, wo_own, wot, wit, g_own,
    pre_part, pre_recv, pre_full, slope, act, dpre,
    hid_own, hid_send, hid_recv,
    top_part, top_send, top_recv, far_part, far_recv, far_send, far_hid,
    top_ss, top_rs, far_ss, far_rs, over_ss, over_rs,
    pass_ss, pass_rs, on_ss, on_rs,
    load_sem, bulk_ss, bulk_rs, pre_ss, pre_rs, full_ss, full_rs,
    hid_ss, hid_rs, g_ss, g_rs, gx_ss, gx_rs, dx_ss, dx_rs,
):
    rows, width = x_own.shape
    own = wi_own.shape[1]
    count = rows // STEP
    share = rows // parts
    section = lax.axis_index("pipe")
    me = lax.axis_index("tensor")
    first = section == pipes - 1
    last = section == 0
    below = jnp.maximum(section - 1, 0)
    above = jnp.minimum(section + 1, pipes - 1)
    peers = [lax.rem(me + d, parts) for d in range(1, parts)]
    other = 1 - lax.axis_index("dp")
    partner = {"dp": other}

    barrier = pltpu.get_barrier_semaphore()
    for peer in peers:
        pl.semaphore_signal(barrier, inc=1, device_id={"tensor": peer}, device_id_type=MESH)
    pl.semaphore_signal(barrier, inc=1, device_id=partner, device_id_type=MESH)

    @pl.when(first)
    def _():
        for peer in peers:
            pl.semaphore_signal(
                barrier, inc=1, device_id={"dp": other, "tensor": peer}, device_id_type=MESH
            )

    @pl.when(section > 0)
    def _():
        pl.semaphore_signal(barrier, inc=1, device_id={"pipe": below}, device_id_type=MESH)

    @pl.when(section < pipes - 1)
    def _():
        pl.semaphore_signal(barrier, inc=1, device_id={"pipe": above}, device_id_type=MESH)

    loads = [
        pltpu.make_async_copy(src, dst, load_sem.at[i])
        for i, (src, dst) in enumerate([(x_hbm, x_own), (wi_hbm, wi_own), (wo_hbm, wo_own), (top_hbm, g_own)])
    ]
    for copy in loads[:3]:
        copy.start()

    @pl.when(first)
    def _():
        loads[3].start()

    beside = jnp.minimum(section, 1) + jnp.minimum(pipes - 1 - section, 1)
    pl.semaphore_wait(barrier, parts + beside + jnp.where(first, parts - 1, 0))

    wi_copy = remote(wi_hbm, wi_other, bulk_ss.at[0], bulk_rs.at[0], partner)
    wo_copy = remote(wot.at[0], wot.at[1], bulk_ss.at[1], bulk_rs.at[1], partner)
    x_copy = remote(x_hbm, x_other, bulk_ss.at[2], bulk_rs.at[2], partner)
    my_share = pl.ds(pl.multiple_of(me * share, share), share)
    act_copy = remote(act.at[1, my_share], act_other.at[my_share], bulk_ss.at[3], bulk_rs.at[3], partner)
    pass_copies = [
        remote(act_other.at[my_share], act_other.at[my_share], pass_ss.at[d], pass_rs.at[d], {"tensor": peer})
        for d, peer in enumerate(peers)
    ]
    wi_copy.start()

    loads[2].wait()

    def turn_out(b, carry):
        cols = pl.ds(pl.multiple_of(b * 256, 256), 256)
        wot[0, cols, :] = wo_own[:, cols].T
        return carry

    lax.fori_loop(0, width // 256, turn_out, 0)

    @pl.when(section < pipes - 1)
    def _():
        wo_copy.start()
        x_copy.start()

    tile = 512
    tiles = width // tile
    group = tiles * STEP

    def rows_of(k):
        return pl.ds(pl.multiple_of(k * STEP, STEP), STEP)

    def g_copy(k):
        return remote(back_ref.at[rows_of(k)], g_own.at[rows_of(k)], g_ss.at[k], g_rs.at[k], {"pipe": below})

    def gx_copy(k):
        return remote(g_own.at[rows_of(k)], g_other.at[rows_of(k)], gx_ss.at[k], gx_rs.at[k], partner)

    def dx_copy(k):
        return remote(dpre.at[1, rows_of(k)], dpre_other.at[rows_of(k)], dx_ss.at[k], dx_rs.at[k], partner)

    def sends_dx(k):
        return (k >= count - tiles) | (lax.rem(k, parts) == me)

    def dx_start(k):
        @pl.when(sends_dx(k))
        def _():
            dx_copy(k).start()

    def on_copies(k):
        r = rows_of(k)
        return [
            remote(dpre_other.at[r], dpre_other.at[r], on_ss.at[k, d], on_rs.at[k, d], {"tensor": peer})
            for d, peer in enumerate(peers)
        ]

    def hid_copies(k):
        return [
            remote(hid_send.at[k], hid_recv.at[k, d], hid_ss.at[k, d], hid_rs.at[k, d], {"tensor": peer})
            for d, peer in enumerate(peers)
        ]

    per_batch = BATCH // STEP
    batch = BATCH
    piece = batch // parts
    batches = rows // batch

    def span(j, size):
        return pl.ds(pl.multiple_of(j * size, size), size)

    def top_copies():
        return [
            remote(top_send, top_recv.at[d], top_ss.at[d], top_rs.at[d], {"tensor": peer})
            for d, peer in enumerate(peers)
        ]

    def far_copies(j):
        return [
            remote(
                far_part.at[j, pl.ds(peer * piece, piece)], far_recv.at[j, d],
                far_ss.at[j, d], far_rs.at[j, d], {"tensor": peer},
            )
            for d, peer in enumerate(peers)
        ]

    def over_copies(j):
        return [
            remote(
                far_send.at[j], far_hid.at[j, d],
                over_ss.at[j, d], over_rs.at[j, d], {"dp": other, "tensor": peer},
            )
            for d, peer in enumerate([me] + peers)
        ]

    def send_top(j):
        for i in range(per_batch):
            gx_copy(per_batch * j + i).start()

    def far_start(j):
        for i in range(per_batch):
            gx_copy(per_batch * j + i).wait_recv()
        far_part[j] = mm(g_other[span(j, batch), :], wot[0])
        for copy in far_copies(j):
            copy.start()

    def far_sum(j):
        for copy in far_copies(j):
            copy.wait_recv()
        total = far_part[j, pl.ds(pl.multiple_of(me * piece, piece), piece), :]
        for d in range(parts - 1):
            total = total + far_recv[j, d]
        half = own // 2
        far_send[j] = jnp.concatenate([total[:, :half], total[:, half:]], axis=0).astype(jnp.bfloat16)
        for copy in over_copies(j):
            copy.start()

    def far_end(j):
        for copy in over_copies(j):
            copy.wait_recv()
        r = span(j, batch)
        near = top_part[r, :]
        for d in range(parts - 1):
            near = near + top_recv[d, r, :].astype(jnp.float32)
        total = g_own[r, :].astype(jnp.float32)
        slice_d = (near * slope[0, r, :]).astype(jnp.bfloat16)
        dpre[0, r, :] = slice_d
        total = total + mm(slice_d, wit[0])
        parts_now = []
        for t in range(parts):
            d = lax.rem(me - t + parts, parts)
            got = far_hid[j, d].astype(jnp.float32)
            parts_now.append(jnp.concatenate([got[:piece], got[piece:]], axis=1))
        slice_d = (jnp.concatenate(parts_now, axis=0) * slope[1, r, :]).astype(jnp.bfloat16)
        dpre[1, r, :] = slice_d
        total = total + mm(slice_d, wit[1])
        back_ref[r, :] = total.astype(jnp.bfloat16)
        for i in range(per_batch):
            g_copy(per_batch * j + i).start()
            dx_start(per_batch * j + i)

    def pre_copies(h):
        return [
            remote(
                pre_part.at[h, pl.ds(peer * share, share)], pre_recv.at[h, d],
                pre_ss.at[h, d], pre_rs.at[h, d], {"tensor": peer},
            )
            for d, peer in enumerate(peers)
        ]

    def full_copies(h):
        mine = pl.ds(me * share, share)
        return [
            remote(
                pre_full.at[h, mine], pre_full.at[h, mine],
                full_ss.at[h, d], full_rs.at[h, d], {"tensor": peer},
            )
            for d, peer in enumerate(peers)
        ]

    def turn_in(h, src):
        def body(b, carry):
            cols = pl.ds(pl.multiple_of(b * 256, 256), 256)
            wit[h, :, cols] = src[cols, :].T
            return carry

        lax.fori_loop(0, width // 256, body, 0)

    def pre_start(h, src):
        pre_part[h] = mm(x_own[...], src[...])
        for copy in pre_copies(h):
            copy.start()

    def pre_sum(h):
        for copy in pre_copies(h):
            copy.wait_recv()
        mine = pl.ds(pl.multiple_of(me * share, share), share)
        total = pre_part[h, mine, :]
        for d in range(parts - 1):
            total = total + pre_recv[h, d]
        pre_full[h, mine, :] = total
        for copy in full_copies(h):
            copy.start()

    def pre_end(h):
        for copy in full_copies(h):
            copy.wait_recv()
        value = pre_full[h]
        slope[h] = silu_slope(value)
        act[h] = jax.nn.silu(value).astype(jnp.bfloat16)

    @pl.when(first)
    def _():
        loads[3].wait()

        for j in range(AHEAD):
            send_top(j)
        near = mm(g_own[...], wot[0])
        top_part[...] = near
        top_send[...] = near.astype(jnp.bfloat16)
        for copy in top_copies():
            copy.start()

    loads[0].wait()
    loads[1].wait()
    pre_start(0, wi_own)
    turn_in(0, wi_own)
    pre_sum(0)
    pre_end(0)
    wi_copy.wait_recv()
    pre_start(1, wi_other)
    turn_in(1, wi_other)
    pre_sum(1)

    @pl.when(first)
    def _():
        far_start(0)
        send_top(AHEAD)
        for copy in top_copies():
            copy.wait_recv()

    pre_end(1)

    @pl.when(first)
    def _():
        def steps(j, carry):
            @pl.when(j < batches)
            def _():
                far_start(j)

                @pl.when(j + AHEAD < batches)
                def _():
                    send_top(j + AHEAD)

            @pl.when(j <= batches)
            def _():
                far_sum(j - 1)

            @pl.when(j >= 2)
            def _():
                far_end(j - 2)

            return carry

        lax.fori_loop(1, batches + 2, steps, 0)
        x_copy.start()
        act_copy.start()

    def hidden_now(k):
        g_copy(k).wait_recv()
        g_now = g_own[rows_of(k), :]
        for h in range(2):
            part = mm(g_now, wot[h])
            hid_own[k, h] = part
            hid_send[k, h] = part.astype(jnp.bfloat16)
        for copy in hid_copies(k):
            copy.start()
        gx_copy(k).start()

    def back_now(k):
        for copy in hid_copies(k):
            copy.wait_recv()
        total = g_own[rows_of(k), :].astype(jnp.float32)
        for h in range(2):
            hidden = hid_own[k, h]
            for d in range(parts - 1):
                hidden = hidden + hid_recv[k, d, h].astype(jnp.float32)
            slice_d = (hidden * slope[h, rows_of(k), :]).astype(jnp.bfloat16)
            dpre[h, rows_of(k), :] = slice_d
            total = total + mm(slice_d, wit[h])
        back_ref[rows_of(k), :] = total.astype(jnp.bfloat16)

        @pl.when(section > 0)
        def _():
            g_copy(k).start()

        dx_start(k)

    near, early = pl.ds(0, rows // 2), pl.ds(0, rows - group)
    rest, late = pl.ds(rows // 2, rows // 2), pl.ds(rows - group, group)
    near_tiles = count // 2
    near_tile = width // near_tiles

    def own_tile(c):
        cols = span(c, near_tile)
        gin_acc[cols, :] = dot(x_own[near, cols], dpre[0, near, :], FIRST)
        gout_acc[:, cols] = dot(act[0, near, :], g_own[near, cols], FIRST)

    def chain(k, carry):
        @pl.when(k < count)
        def _():
            hidden_now(k)

        done = k - LAG

        @pl.when(done >= 0)
        def _():
            back_now(done)

        @pl.when(done >= count - near_tiles)
        def _():
            own_tile(done - (count - near_tiles))

        @pl.when(done == count - 2)
        def _():
            act_copy.wait_recv()
            for copy in pass_copies:
                copy.start()

        return carry

    @pl.when(section < pipes - 1)
    def _():
        act_copy.start()
        wo_copy.wait_recv()
        lax.fori_loop(0, count + LAG, chain, 0)

    @pl.when(first)
    def _():
        def all_own(c, carry):
            own_tile(c)
            return carry

        lax.fori_loop(0, near_tiles, all_own, 0)
        act_copy.wait_recv()
        for copy in pass_copies:
            copy.start()

    def move_on(i, carry):
        k = i * parts + me
        dx_copy(k).wait_recv()
        for copy in on_copies(k):
            copy.start()
        return carry

    lax.fori_loop(0, (count - tiles) // parts, move_on, 0)
    for copy in pass_copies:
        copy.wait_recv()

    def wait_gx(k, carry):
        gx_copy(k).wait_recv()
        return carry

    def wait_dx(k, carry):
        dx_copy(k).wait_recv()
        return carry

    @pl.when(section < pipes - 1)
    def _():
        lax.fori_loop(0, count - tiles, wait_gx, 0)

    def early_tile(c, carry):
        cols = span(c, tile)
        far_out = dot(act_other[early, :], g_other[early, cols], FIRST)
        gout_acc[:, cols] += dot(act[0, rest, :], g_own[rest, cols], FIRST) + far_out
        return carry

    lax.fori_loop(0, tiles, early_tile, 0)
    x_copy.wait_recv()

    def wait_on(k, carry):
        source = lax.rem(k, parts)

        @pl.when(source != me)
        def _():
            d = lax.rem(me - source + parts, parts) - 1
            r = rows_of(k)
            remote(dpre_other.at[r], dpre_other.at[r], on_ss.at[k, d], on_rs.at[k, d], partner).wait_recv()

        return carry

    lax.fori_loop(0, count - tiles, wait_on, 0)

    def early_in(c, carry):
        cols = span(c, tile)
        far_in = dot(x_other[early, cols], dpre_other[early, :], FIRST)
        gin_acc[cols, :] += dot(x_own[rest, cols], dpre[0, rest, :], FIRST) + far_in
        return carry

    lax.fori_loop(0, tiles, early_in, 0)

    for copy in [wi_copy, x_copy, act_copy] + pass_copies:
        copy.wait_send()

    @pl.when(section < pipes - 1)
    def _():
        wo_copy.wait_send()

    @pl.when(first)
    def _():
        for copy in top_copies():
            copy.wait_send()

        def drain_far(j, carry):
            for copy in far_copies(j) + over_copies(j):
                copy.wait_send()
            return carry

        lax.fori_loop(0, batches, drain_far, 0)

    for h in range(2):
        for copy in pre_copies(h) + full_copies(h):
            copy.wait_send()

    def sent_x(k, carry):
        gx_copy(k).wait_send()

        @pl.when(sends_dx(k))
        def _():
            dx_copy(k).wait_send()

        return carry

    def drain(k, carry):
        @pl.when((k < count - tiles) & (lax.rem(k, parts) == me))
        def _():
            for copy in on_copies(k):
                copy.wait_send()

        @pl.when(section < pipes - 1)
        def _():
            for copy in hid_copies(k):
                copy.wait_send()

        @pl.when(section > 0)
        def _():
            g_copy(k).wait_send()

        return carry

    lax.fori_loop(0, count, drain, 0)
    lax.fori_loop(0, count - tiles, sent_x, 0)

    @pl.when(section < pipes - 1)
    def _():
        lax.fori_loop(count - tiles, count, wait_gx, 0)

    lax.fori_loop(count - tiles, count, wait_dx, 0)

    lax.fori_loop(count - tiles, count, sent_x, 0)


def finish(
    late, tile,
    back_ref, gin_acc, gout_acc, x_other, g_other, act_other, dpre_other,
    back_out, gin_out, gout_out, gin_part, gout_part, sems,
):
    rows, width = x_other.shape
    tiles = width // tile
    r = pl.ds(rows - late, late)
    half = rows // 2
    copies = []
    for j in range(2):
        part = pl.ds(j * half, half)
        copies.append(pltpu.make_async_copy(back_ref.at[part], back_out.at[part], sems.at[0, j]))
        copies[-1].start()
    for c in range(tiles):
        cols = pl.ds(c * tile, tile)
        gin_part[cols, :] = (gin_acc[cols, :] + dot(x_other[r, cols], dpre_other[r, :], FIRST)).astype(jnp.bfloat16)
        copies.append(pltpu.make_async_copy(gin_part.at[cols], gin_out.at[cols], sems.at[1, c]))
        copies[-1].start()
        gout_part[:, cols] = (gout_acc[:, cols] + dot(act_other[r, :], g_other[r, cols], FIRST)).astype(jnp.bfloat16)
        copies.append(pltpu.make_async_copy(gout_part.at[:, cols], gout_out.at[:, cols], sems.at[2, c]))
        copies[-1].start()
    for copy in copies:
        copy.wait()


def written(arrays):
    back, gin, gout = arrays[:3]
    tile = 512
    tiles = back.shape[1] // tile
    bf = jnp.bfloat16
    shapes = (back.shape, gin.shape, gout.shape)
    return pl.pallas_call(
        functools.partial(finish, tiles * STEP, tile),
        out_shape=tuple(jax.ShapeDtypeStruct(shape, bf) for shape in shapes),
        in_specs=[pl.BlockSpec(memory_space=pltpu.VMEM)] * len(arrays),
        out_specs=tuple(pl.BlockSpec(memory_space=pl.ANY) for _ in shapes),
        scratch_shapes=[
            pltpu.VMEM(gin.shape, bf), pltpu.VMEM(gout.shape, bf),
            pltpu.SemaphoreType.DMA((3, tiles)),
        ],
        compiler_params=pltpu.CompilerParams(vmem_limit_bytes=8 * 1024 * 1024),
    )(*arrays)


def pair_call(saved, w_in_now, w_out_now, top):
    pipes = lax.axis_size("pipe")
    parts = lax.axis_size("tensor")
    rows, width = saved.shape
    own = w_in_now.shape[1]
    count = rows // STEP
    share = rows // parts
    batches = rows // BATCH
    piece = BATCH // parts
    others = parts - 1
    bf, f32 = jnp.bfloat16, jnp.float32
    dma = pltpu.SemaphoreType.DMA
    vmem = pl.BlockSpec(memory_space=pltpu.VMEM)
    anywhere = pl.BlockSpec(memory_space=pl.ANY)
    return pl.pallas_call(
        functools.partial(paired, pipes, parts),
        out_shape=(
            jax.ShapeDtypeStruct((rows, width), bf),
            jax.ShapeDtypeStruct((width, own), f32),
            jax.ShapeDtypeStruct((own, width), f32),
            jax.ShapeDtypeStruct((rows, width), bf),
            jax.ShapeDtypeStruct((rows, width), bf),
            jax.ShapeDtypeStruct((rows, own), bf),
            jax.ShapeDtypeStruct((rows, own), bf),
        ),
        in_specs=[anywhere] * 4,
        out_specs=(vmem,) * 7,
        scratch_shapes=[
            pltpu.VMEM((rows, width), bf),
            pltpu.VMEM((width, own), bf),
            pltpu.VMEM((width, own), bf),
            pltpu.VMEM((own, width), bf),
            pltpu.VMEM((2, width, own), bf),
            pltpu.VMEM((2, own, width), bf),
            pltpu.VMEM((rows, width), bf),
            pltpu.VMEM((2, rows, own), f32),
            pltpu.VMEM((2, others, share, own), f32),
            pltpu.VMEM((2, rows, own), f32),
            pltpu.VMEM((2, rows, own), f32),
            pltpu.VMEM((2, rows, own), bf),
            pltpu.VMEM((2, rows, own), bf),
            pltpu.VMEM((count, 2, STEP, own), f32),
            pltpu.VMEM((count, 2, STEP, own), bf),
            pltpu.VMEM((count, others, 2, STEP, own), bf),
            pltpu.VMEM((rows, own), f32),
            pltpu.VMEM((rows, own), bf),
            pltpu.VMEM((others, rows, own), bf),
            pltpu.VMEM((batches, BATCH, own), f32),
            pltpu.VMEM((batches, others, piece, own), f32),
            pltpu.VMEM((batches, 2 * piece, own // 2), bf),
            pltpu.VMEM((batches, parts, 2 * piece, own // 2), bf),
            dma((others,)), dma((others,)),
            dma((batches, others)), dma((batches, others)),
            dma((batches, parts)), dma((batches, parts)),
            dma((others,)), dma((others,)), dma((count, others)), dma((count, others)),
            dma((4,)), dma((4,)), dma((4,)),
            dma((2, others)), dma((2, others)), dma((2, others)), dma((2, others)),
            dma((count, others)), dma((count, others)),
            dma((count,)), dma((count,)), dma((count,)), dma((count,)), dma((count,)), dma((count,)),
        ],
        compiler_params=pltpu.CompilerParams(
            collective_id=0, has_side_effects=True, vmem_limit_bytes=42 * 1024 * 1024
        ),
    )(*[pltpu.with_memory_space_constraint(a, pltpu.HBM) for a in (saved, w_in_now, w_out_now, top)])


def chain(
    pipes, parts, pair, chunks,
    x_ref, wi_ref, wo_ref, top_ref,
    back_ref, pin_ref, pout_ref,
    g_buf, pre_send, pre_recv, act_buf, hid_send, hid_recv, dpre_buf, slope_buf,
    pre_ss, pre_rs, act_ss, act_rs, hid_ss, hid_rs, dp_ss, dp_rs, g_ss, g_rs,
    *across,
):
    micro, rows, width = x_ref.shape
    own = wi_ref.shape[1]
    halves = 2 if pair else 1
    per = parts // halves
    quarter = own // per
    step_w = width // chunks
    section = lax.axis_index("pipe")
    me = lax.axis_index("tensor")
    first = section == pipes - 1
    below = jnp.maximum(section - 1, 0)
    above = jnp.minimum(section + 1, pipes - 1)
    peers = [lax.rem(me + d, parts) for d in range(1, parts)]

    barrier = pltpu.get_barrier_semaphore()
    for peer in peers:
        pl.semaphore_signal(barrier, inc=1, device_id={"tensor": peer}, device_id_type=MESH)
    if pair:
        partner = {"dp": 1 - lax.axis_index("dp")}
        pl.semaphore_signal(barrier, inc=1, device_id=partner, device_id_type=MESH)

    @pl.when(section > 0)
    def _():
        pl.semaphore_signal(barrier, inc=1, device_id={"pipe": below}, device_id_type=MESH)

    @pl.when(section < pipes - 1)
    def _():
        pl.semaphore_signal(barrier, inc=1, device_id={"pipe": above}, device_id_type=MESH)

    beside = jnp.minimum(section, 1) + jnp.minimum(pipes - 1 - section, 1)
    pl.semaphore_wait(barrier, parts - 1 + halves - 1 + beside)

    def remote(src, dst, send, recv, where):
        return pltpu.make_async_remote_copy(
            src_ref=src, dst_ref=dst, send_sem=send, recv_sem=recv,
            device_id=where, device_id_type=MESH,
        )

    wi_halves, wo_halves = [wi_ref], [wo_ref]
    if pair:
        wi_other, wo_other, x_other, g_other, dpre_other, act_other, one_ss, one_rs, gx_ss, gx_rs, dx_ss, dx_rs = across
        wi_halves.append(wi_other)
        wo_halves.append(wo_other)
        wi_copy = remote(wi_ref, wi_other, one_ss.at[0], one_rs.at[0], partner)
        wo_copy = remote(wo_ref, wo_other, one_ss.at[1], one_rs.at[1], partner)
        x_copy = remote(x_ref, x_other, one_ss.at[2], one_rs.at[2], partner)
        actx_copy = remote(act_buf.at[pl.ds(per, per)], act_other, one_ss.at[3], one_rs.at[3], partner)
        gx_copies = [remote(g_buf.at[m], g_other.at[m], gx_ss.at[m], gx_rs.at[m], partner) for m in range(micro)]
        dx_copies = [
            remote(dpre_buf.at[m, pl.ds(per, per)], dpre_other.at[m], dx_ss.at[m], dx_rs.at[m], partner)
            for m in range(micro)
        ]
        wi_copy.start()

    @pl.when(first)
    def _():
        g_buf[...] = top_ref[...]

    pre_copies = [
        remote(pre_send.at[peer], pre_recv.at[d], pre_ss.at[d], pre_rs.at[d], {"tensor": peer})
        for d, peer in enumerate(peers)
    ]
    hid_copies = [
        [
            remote(hid_send.at[m, peer], hid_recv.at[m, d], hid_ss.at[m, d], hid_rs.at[m, d], {"tensor": peer})
            for d, peer in enumerate(peers)
        ]
        for m in range(micro)
    ]
    dp_copies = [
        [
            remote(dpre_buf.at[m, me], dpre_buf.at[m, me], dp_ss.at[m, d], dp_rs.at[m, d], {"tensor": peer})
            for d, peer in enumerate(peers)
        ]
        for m in range(micro)
    ]
    act_copies = [
        remote(act_buf.at[me], act_buf.at[me], act_ss.at[d], act_rs.at[d], {"tensor": peer})
        for d, peer in enumerate(peers)
    ]
    g_copies = [
        [
            remote(
                back_ref.at[m, :, pl.ds(c * step_w, step_w)], g_buf.at[m, :, pl.ds(c * step_w, step_w)],
                g_ss.at[m, c], g_rs.at[m, c], {"pipe": below},
            )
            for c in range(chunks)
        ]
        for m in range(micro)
    ]

    flat_x = x_ref[...].reshape(micro * rows, width)
    for h in range(halves):
        if h == 1:
            wi_copy.wait_recv()
            wo_copy.start()
        pre = jnp.dot(flat_x, wi_halves[h][...], preferred_element_type=jnp.float32)
        for t in range(per):
            pre_send[h * per + t] = pre[:, t * quarter : (t + 1) * quarter]
    for copy in pre_copies:
        copy.start()

    def hidden_now(which):
        count = len(which)
        g_now = g_buf[which[0] : which[-1] + 1].reshape(count * rows, width)
        for h in range(halves):
            part = dot(g_now, wo_halves[h][...], LAST)
            for t in range(per):
                for i, m in enumerate(which):
                    hid_send[m, h * per + t] = part[i * rows : (i + 1) * rows, t * quarter : (t + 1) * quarter]
        for m in which:
            for copy in hid_copies[m]:
                copy.start()
        if pair:
            for m in which:
                gx_copies[m].start()

    def dpre_now(m):
        for copy in hid_copies[m]:
            copy.wait_recv()
        hidden = hid_send[m, me]
        for d in range(parts - 1):
            hidden = hidden + hid_recv[m, d]
        dpre_buf[m, me] = (hidden * slope_buf[m * rows : (m + 1) * rows, :]).astype(jnp.bfloat16)
        for copy in dp_copies[m]:
            copy.start()

    for copy in pre_copies:
        copy.wait_recv()
    mine = pre_send[me]
    for d in range(parts - 1):
        mine = mine + pre_recv[d]
    slope_buf[...] = silu_slope(mine)
    act_buf[me] = jax.nn.silu(mine).astype(jnp.bfloat16)
    for copy in act_copies:
        copy.start()

    if pair:
        wo_copy.wait_recv()
        x_copy.start()

    @pl.when(first)
    def _():
        hidden_now(list(range(micro)))
        for m in range(micro):
            dpre_now(m)

    for m in range(micro):
        @pl.when(section < pipes - 1)
        def _():
            for copy in g_copies[m]:
                copy.wait_recv()
            hidden_now([m])
            dpre_now(m)

        for copy in dp_copies[m]:
            copy.wait_recv()
        dpre_halves = [
            jnp.concatenate([dpre_buf[m, h * per + t] for t in range(per)], axis=1) for h in range(halves)
        ]
        for c in range(chunks):
            cols = pl.ds(c * step_w, step_w)
            total = g_buf[m, :, cols].astype(jnp.float32)
            for h in range(halves):
                total = total + dot(dpre_halves[h], wi_halves[h][cols, :], LAST)
            back_ref[m, :, cols] = total.astype(jnp.bfloat16)

            @pl.when(section > 0)
            def _():
                g_copies[m][c].start()

        if pair:
            dx_copies[m].start()
        if m == 0:
            for copy in act_copies:
                copy.wait_recv()
            if pair:
                actx_copy.start()

    sources = [(x_ref, g_buf, act_buf, dpre_buf)]
    if pair:
        x_copy.wait_recv()
        actx_copy.wait_recv()
        for m in range(micro):
            gx_copies[m].wait_recv()
            dx_copies[m].wait_recv()
        sources.append((x_other, g_other, act_other, dpre_other))
    ready = []
    for x_from, g_from, act_from, dpre_from in sources:
        act = jnp.concatenate([act_from[t] for t in range(per)], axis=1)
        dpre = jnp.concatenate(
            [dpre_from[:, t].reshape(micro * rows, quarter) for t in range(per)], axis=1
        )
        ready.append((x_from, g_from, act, dpre))

    for c in range(chunks):
        cols = pl.ds(c * step_w, step_w)
        grad_in, grad_out = 0.0, 0.0
        for x_from, g_from, act, dpre in ready:
            x_cols = x_from[:, :, cols].reshape(micro * rows, step_w)
            g_cols = g_from[:, :, cols].reshape(micro * rows, step_w)
            grad_in = grad_in + dot(x_cols, dpre, FIRST)
            grad_out = grad_out + dot(act, g_cols, FIRST)
        pin_ref[cols, :] = grad_in.astype(jnp.bfloat16)
        pout_ref[:, cols] = grad_out.astype(jnp.bfloat16)

    for copy in pre_copies + act_copies:
        copy.wait_send()
    if pair:
        for copy in [wi_copy, wo_copy, x_copy, actx_copy] + gx_copies + dx_copies:
            copy.wait_send()
    for m in range(micro):
        for copy in hid_copies[m] + dp_copies[m]:
            copy.wait_send()

        @pl.when(section > 0)
        def _():
            for copy in g_copies[m]:
                copy.wait_send()


def shards(acts, w_in, w_out, top_grad):
    pipes = lax.axis_size("pipe")
    parts = lax.axis_size("tensor")
    pair = lax.axis_size("dp") == 2 and parts % 2 == 0
    saved = acts[0]
    micro, rows, width = saved.shape
    if pair:
        out = written(pair_call(
            saved.reshape(micro * rows, width), w_in[0], w_out[0], top_grad.reshape(micro * rows, width)
        ))
        return out[0].reshape(1, micro, rows, width), out[1][None], out[2][None]
    if pair:
        w_in_now, w_out_now = w_in[0], w_out[0]
    else:
        w_in_now = lax.all_gather(w_in[0], "dp", axis=1, tiled=True)
        w_out_now = lax.all_gather(w_out[0], "dp", axis=0, tiled=True)
    own = w_in_now.shape[1]
    per = parts // 2 if pair else parts
    quarter = own // per
    chunks = 4
    others = parts - 1
    bf, f32 = jnp.bfloat16, jnp.float32
    dma = pltpu.SemaphoreType.DMA
    vmem = pl.BlockSpec(memory_space=pltpu.VMEM)
    across = []
    if pair:
        across = [
            pltpu.VMEM((width, own), bf),
            pltpu.VMEM((own, width), bf),
            pltpu.VMEM((micro, rows, width), bf),
            pltpu.VMEM((micro, rows, width), bf),
            pltpu.VMEM((micro, per, rows, quarter), bf),
            pltpu.VMEM((per, micro * rows, quarter), bf),
            dma((4,)), dma((4,)),
            dma((micro,)), dma((micro,)), dma((micro,)), dma((micro,)),
        ]
    back, grad_in, grad_out = pl.pallas_call(
        functools.partial(chain, pipes, parts, pair, chunks),
        out_shape=(
            jax.ShapeDtypeStruct((micro, rows, width), bf),
            jax.ShapeDtypeStruct((width, own), bf),
            jax.ShapeDtypeStruct((own, width), bf),
        ),
        in_specs=[vmem] * 4,
        out_specs=(vmem,) * 3,
        scratch_shapes=[
            pltpu.VMEM((micro, rows, width), bf),
            pltpu.VMEM((parts, micro * rows, quarter), f32),
            pltpu.VMEM((others, micro * rows, quarter), f32),
            pltpu.VMEM((parts, micro * rows, quarter), bf),
            pltpu.VMEM((micro, parts, rows, quarter), f32),
            pltpu.VMEM((micro, others, rows, quarter), f32),
            pltpu.VMEM((micro, parts, rows, quarter), bf),
            pltpu.VMEM((micro * rows, quarter), f32),
            dma((others,)), dma((others,)), dma((others,)), dma((others,)),
            dma((micro, others)), dma((micro, others)),
            dma((micro, others)), dma((micro, others)),
            dma((micro, chunks)), dma((micro, chunks)),
            *across,
        ],
        compiler_params=pltpu.CompilerParams(
            collective_id=0, has_side_effects=True, vmem_limit_bytes=48 * 1024 * 1024
        ),
    )(saved, w_in_now, w_out_now, top_grad)
    if not pair:
        grad_in = lax.psum_scatter(grad_in, "dp", scatter_dimension=1, tiled=True)
        grad_out = lax.psum_scatter(grad_out, "dp", scatter_dimension=0, tiled=True)
    return back[None], grad_in[None], grad_out[None]


def solution(mesh):
    placed = (
        P("pipe", None, "dp", "tensor"),
        P("pipe", "tensor", "dp"),
        P("pipe", "dp", "tensor"),
        P(None, "dp", "tensor"),
    )
    return jax.shard_map(
        shards,
        mesh=mesh,
        in_specs=placed,
        out_specs=(
            P("pipe", None, "dp", "tensor"),
            P("pipe", "tensor", "dp"),
            P("pipe", "dp", "tensor"),
        ),
        check_vma=False,
    )
```
